256 devices in a mesh: dp: 8 (over z_hi, x), mp: 32 (over y, z_lo, core).
Axes of the slice: x: 4, y: 4, z: 8 (z_hi: 2, z_lo: 4; z = z_hi * 4 + z_lo), core: 2. Of those that a mesh axis runs over, the one named last changes fastest.
Arguments:
- tokens: bfloat16 [1024, 8192], P('dp', 'mp'), may hold values from -6 to 6
- gate_weight: bfloat16 [8192, 14336], P('mp', 'dp'), may hold values from -0.0625 to 0.0625
- up_weight: bfloat16 [8192, 14336], P('mp', 'dp'), may hold values from -0.0625 to 0.0625
- down_weight: bfloat16 [14336, 8192], P('dp', 'mp'), may hold values from -0.046875 to 0.046875
- factor_self: bfloat16 [5, 8192, 256], P(None, 'mp'), may hold values from -0.25 to 0.25
- factor_cross: bfloat16 [5, 8192, 256], P(None, 'mp'), may hold values from -0.25 to 0.25
- cotangent: bfloat16 [1024, 8192], P('dp', 'mp'), may hold values from -1.1953125 to 1.1953125
Outputs:
- mixed_out: bfloat16 [1024, 8192], P('dp', 'mp')
- input_grad: bfloat16 [1024, 8192], P('dp', 'mp')
- self_grad: float32 [5, 8192, 256], P(None, 'mp')
- cross_grad: float32 [5, 8192, 256], P(None, 'mp')
The draws below stay inside these ranges and needn't reach their ends.
All inputs are finite; a program needn't handle non-finite values.
Results may differ from the reference program's by a relative error of at most 0.04.
Values may be sent and summed in bfloat16 or wider, within the bound.
No kernel may reach another device: no remote copies, remote signals or barrier semaphores. Data moves between devices by JAX's collectives and lax.ppermute only.
A program may use at most 128 MiB of HBM per device.

```python
import jax
import jax.numpy as jnp
from jax import lax

D = 8192
FF = 14336
BLOCK = 256
SECTIONS = 5
TOKENS = 1024
N_MP = 32


def level_of(key, extent, pieces, least, high):
    def one(axis_at, blocks):
        draws = jax.random.uniform(jax.random.fold_in(jax.random.fold_in(key, 6), axis_at), (blocks,), jnp.float32, least / len(pieces), high / len(pieces))
        return jnp.repeat(jnp.exp(draws), extent[axis_at] // blocks).reshape((-1,) + (1,) * (len(extent) - axis_at - 1))

    factor_of = one(*pieces[0])
    for cut in pieces[1:]:
        factor_of = factor_of * one(*cut)
    return factor_of


def centred(key, extent, deviation, bound, shards=(), kind=jnp.bfloat16):
    entries = deviation * jax.random.normal(key, extent, jnp.float32)
    if shards:
        entries = entries * level_of(key, extent, shards, -0.22, 0.18)
    return jnp.clip(entries, -bound, bound).astype(kind)


def setup_inputs(seed: int = 0) -> dict:
    key_of = jax.random.split(jax.random.key(seed), 8)
    tokens = centred(key_of[0], (TOKENS, D), 1.0, 6.0, ((0, 8), (1, 32)))
    gate_weight = centred(key_of[1], (D, FF), D ** -0.5, 0.0625, ((0, 32), (1, 8)))
    up_weight = centred(key_of[2], (D, FF), D ** -0.5, 0.0625, ((0, 32), (1, 8)))
    down_weight = centred(key_of[3], (FF, D), FF ** -0.5, 0.046875, ((0, 8), (1, 32)))
    factor_self = centred(key_of[4], (SECTIONS, D, BLOCK), (2 * BLOCK) ** -0.5, 0.25, ((1, 32),))
    factor_cross = centred(key_of[5], (SECTIONS, D, BLOCK), (2 * BLOCK) ** -0.5, 0.25, ((1, 32),))
    cotangent = centred(key_of[6], (TOKENS, D), 0.2, 1.1953125, ((0, 8), (1, 32)))
    return {"tokens": tokens, "gate_weight": gate_weight, "up_weight": up_weight, "down_weight": down_weight, "factor_self": factor_self, "factor_cross": factor_cross, "cotangent": cotangent}


def partner_blocks(blocks, degree):
    tok_rows, amount, breadth = blocks.shape
    distance = 2 ** degree
    folded = blocks.reshape(tok_rows, amount // (2 * distance), 2, distance, breadth)
    return jnp.flip(folded, 2).reshape(tok_rows, amount, breadth)


def grouped(left_side, right_side):
    group_rows = D // N_MP

    def add_group(running, group_idx):
        start_at = (group_idx * group_rows).astype(jnp.int32)
        left_part = lax.dynamic_slice_in_dim(left_side, start_at, group_rows, 1)
        right_part = lax.dynamic_slice_in_dim(right_side, start_at, group_rows, 0)
        portion = jnp.dot(left_part, right_part, preferred_element_type=jnp.float32)
        portion = lax.optimization_barrier(portion.astype(jnp.bfloat16)).astype(jnp.float32)
        return running + portion, None

    initial = jnp.zeros((left_side.shape[0], right_side.shape[1]), jnp.float32)
    running, _ = lax.scan(add_group, initial, jnp.arange(N_MP, dtype=jnp.int32))
    return running


def reference(tokens, gate_weight, up_weight, down_weight, factor_self, factor_cross, cotangent):
    amount = D // BLOCK
    highest = lax.Precision.HIGHEST
    current = tokens.reshape(TOKENS, amount, BLOCK)
    inputs = []
    partners = []
    for degree in range(SECTIONS):
        self_mat = factor_self[degree].reshape(amount, BLOCK, BLOCK).astype(jnp.float32)
        cross_mat = factor_cross[degree].reshape(amount, BLOCK, BLOCK).astype(jnp.float32)
        partner = partner_blocks(current, degree)
        inputs.append(current)
        partners.append(partner)
        result = jnp.einsum('tkb,kbc->tkc', current.astype(jnp.float32), self_mat, precision=highest)
        result = result + jnp.einsum('tkb,kbc->tkc', partner.astype(jnp.float32), cross_mat, precision=highest)
        current = result.astype(jnp.bfloat16)
    rotated = current.reshape(TOKENS, D)
    gate_sum = grouped(rotated, gate_weight)
    up_sum = grouped(rotated, up_weight)
    hidden = (jax.nn.silu(gate_sum) * up_sum).astype(jnp.bfloat16)
    mixed_out = jnp.dot(hidden, down_weight, preferred_element_type=jnp.float32).astype(jnp.bfloat16)
    hidden_grad = grouped(cotangent, down_weight.T)
    logistic = jax.nn.sigmoid(gate_sum)
    gate_grad = (hidden_grad * up_sum * logistic * (1.0 + gate_sum * (1.0 - logistic))).astype(jnp.bfloat16)
    up_grad = (hidden_grad * gate_sum * logistic).astype(jnp.bfloat16)
    rotated_grad = jnp.dot(gate_grad, gate_weight.T, preferred_element_type=jnp.float32)
    rotated_grad = rotated_grad + jnp.dot(up_grad, up_weight.T, preferred_element_type=jnp.float32)
    gradient = rotated_grad.astype(jnp.bfloat16).reshape(TOKENS, amount, BLOCK)
    self_list = [None] * SECTIONS
    cross_list = [None] * SECTIONS
    for degree in reversed(range(SECTIONS)):
        self_mat = factor_self[degree].reshape(amount, BLOCK, BLOCK).astype(jnp.float32)
        cross_mat = factor_cross[degree].reshape(amount, BLOCK, BLOCK).astype(jnp.float32)
        grad_f = gradient.astype(jnp.float32)
        self_list[degree] = jnp.einsum('tkb,tkc->kbc', inputs[degree].astype(jnp.float32), grad_f, precision=highest).reshape(D, BLOCK)
        cross_list[degree] = jnp.einsum('tkb,tkc->kbc', partners[degree].astype(jnp.float32), grad_f, precision=highest).reshape(D, BLOCK)
        direct = jnp.einsum('tkc,kbc->tkb', grad_f, self_mat, precision=highest)
        carried = jnp.einsum('tkc,kbc->tkb', grad_f, cross_mat, precision=highest)
        gradient = (direct + partner_blocks(carried, degree)).astype(jnp.bfloat16)
    input_grad = gradient.reshape(TOKENS, D)
    return mixed_out, input_grad, jnp.stack(self_list), jnp.stack(cross_list)
```

```python
import jax
import jax.numpy as jnp
from jax import lax
from jax.sharding import Mesh
from jax.sharding import PartitionSpec as P

BLOCK = 256
SECTIONS = 5
DP = ("h", "x")
MP = ("y", "lh", "ll", "c")
BF = jnp.bfloat16
F32 = jnp.float32
PARTNER = (("c", 1), ("ll", 1), ("lh", 1), ("y", 1), ("y", 2))


def swap(value, axis, bits=1):
    count = lax.axis_size(axis)
    return lax.ppermute(value, axis, [(i, i ^ bits) for i in range(count)])


def pick(value, index):
    return lax.dynamic_index_in_dim(value, index, 0, keepdims=False)


def dot(a, b):
    return jnp.dot(a, b, preferred_element_type=F32)


def dot_t(a, b):
    return lax.dot_general(a, b, (((1,), (1,)), ((), ())), preferred_element_type=F32)


def t_dot(a, b):
    return lax.dot_general(a, b, (((0,), (0,)), ((), ())), preferred_element_type=F32)


def f32(v):
    return v.astype(F32)


def gather4(value, axis):
    return jnp.stack([value] + [swap(value, axis, k) for k in (1, 2, 3)])


def scatter4(parts, axis, order):
    sent = [swap(pick(parts, order ^ k), axis, k) for k in (1, 2, 3)]
    total = f32(pick(parts, order))
    for v in sent:
        total = total + f32(v)
    return total


def halves(parts, axis, mine):
    other = swap(pick(parts, 1 - mine).astype(BF), axis)
    return pick(parts, mine) + f32(other)


def by_pair(own, other, index):
    return jnp.stack([jnp.where(index == 0, own, other), jnp.where(index == 0, other, own)])


def per_device(tokens, gate_weight, up_weight, down_weight, factor_self, factor_cross, cotangent):
    h, x, y, lh, ll, c = (lax.axis_index(a) for a in (*DP, *MP))
    rel_h = lh ^ h
    rel_xy = x ^ y
    rows = tokens.shape[0]
    n = rows // 4

    def paired(weight):
        far = swap(weight, "ll")
        return [weight, swap(weight, "c"), far, swap(far, "c")]

    gates = paired(gate_weight)
    ups = paired(up_weight)
    weight = jnp.concatenate(
        [jnp.concatenate(gates, axis=0), jnp.concatenate(ups, axis=0)], axis=1
    )
    down = jnp.concatenate([down_weight, swap(down_weight, "c")], axis=1)
    ff = gate_weight.shape[1]

    halved = cotangent.reshape(2, rows // 2, BLOCK)
    cot = jnp.concatenate([pick(halved, c), swap(pick(halved, 1 - c), "c")], axis=1)
    cot = jnp.stack([cot, swap(cot, "h")])
    cot = gather4(cot, "x").reshape(-1, 2 * BLOCK)

    current = tokens
    inputs = []
    partners = []
    for degree in range(SECTIONS):
        axis, bits = PARTNER[degree]
        partner = swap(current, axis, bits)
        inputs.append(current)
        partners.append(partner)
        result = dot(current, factor_self[degree]) + dot(partner, factor_cross[degree])
        current = result.astype(BF)

    terms = dot_t(cot, down).astype(BF)
    hid = scatter4(terms.reshape(4, -1, ff), "y", rel_xy)
    hid = hid.reshape(2, 2, n, ff)
    hid = jnp.moveaxis(hid, 1, 0).reshape(2, 2 * n, ff)
    hid = halves(hid, "ll", ll).reshape(2, n, ff)
    hidden_grad = halves(hid, "lh", rel_h)

    quarters = current.reshape(2, 2, n, BLOCK)

    def quarter(dc, dl):
        return pick(pick(quarters, c ^ dc), ll ^ dl)

    mine = jnp.concatenate(
        [
            quarter(0, 0),
            swap(quarter(1, 0), "c"),
            swap(quarter(0, 1), "ll"),
            swap(quarter(1, 1), ("ll", "c"), 3),
        ],
        axis=1,
    )
    mine = jnp.stack([mine, swap(mine, "h")])
    rotated = gather4(mine, "x").reshape(-1, 4 * BLOCK)

    sums = dot(rotated, weight).astype(BF)
    sums = scatter4(sums.reshape(4, 2 * n, 2 * ff), "y", rel_xy)
    sums = halves(sums.reshape(2, n, 2 * ff), "lh", rel_h)
    gate_sum = sums[:, :ff]
    up_sum = sums[:, ff:]

    logistic = jax.nn.sigmoid(gate_sum)
    silu = gate_sum * logistic
    hidden = (silu * up_sum).astype(BF)
    gate_grad = hidden_grad * up_sum * logistic * (1.0 + gate_sum * (1.0 - logistic))
    up_grad = hidden_grad * gate_sum * logistic
    grads = jnp.concatenate([gate_grad.astype(BF), up_grad.astype(BF)], axis=1)

    grads = jnp.stack([grads, swap(grads, "lh")])
    grads = gather4(grads, "y").reshape(-1, 2 * ff)
    terms = dot_t(grads, weight).astype(BF)

    hidden, terms = lax.optimization_barrier((hidden, terms))
    hidden = jnp.stack([hidden, swap(hidden, "lh")])
    hidden = jnp.stack([hidden, swap(hidden, "ll")])
    hidden = gather4(hidden, "y").reshape(-1, ff)

    total = scatter4(terms.reshape(4, 2 * n, 4 * BLOCK), "x", rel_xy)
    total = halves(total.reshape(2, n, 4 * BLOCK), "h", rel_h).astype(BF)
    blocks = [total[:, i * BLOCK : (i + 1) * BLOCK] for i in range(4)]
    near = by_pair(blocks[0], swap(blocks[2], "ll"), ll)
    far = by_pair(swap(blocks[1], "c"), swap(blocks[3], ("ll", "c"), 3), ll)
    gradient = by_pair(near, far, c).reshape(rows, BLOCK)

    def summed(batch):
        parts = jnp.stack(batch).astype(BF)
        count = parts.shape[0]
        parts = jnp.moveaxis(parts.reshape(count, 4, BLOCK // 4, BLOCK), 1, 0)
        part = scatter4(parts.reshape(4, -1, BLOCK), "x", x).astype(BF)
        part = (f32(part) + f32(swap(part, "h"))).astype(BF)
        whole = gather4(part, "x")
        whole = jnp.stack([pick(whole, x ^ k) for k in range(4)])
        whole = jnp.moveaxis(whole.reshape(4, count, BLOCK // 4, BLOCK), 0, 1)
        return f32(whole).reshape(count, BLOCK, BLOCK)

    self_list = [None] * SECTIONS
    cross_list = [None] * SECTIONS
    batch = []
    members = []
    for degree in reversed(range(SECTIONS)):
        axis, bits = PARTNER[degree]
        carried = dot_t(gradient, factor_cross[degree]).astype(BF)
        returned = swap(carried, axis, bits)
        batch += [t_dot(inputs[degree], gradient), t_dot(partners[degree], gradient)]
        members.append(degree)
        if degree in (3, 1, 0):
            out = summed(batch)
            for i, d in enumerate(members):
                self_list[d] = out[2 * i]
                cross_list[d] = out[2 * i + 1]
            batch = []
            members = []
        direct = dot_t(gradient, factor_self[degree])
        gradient = (direct + f32(returned)).astype(BF)

    terms = dot(hidden, down).astype(BF)
    mixed = scatter4(terms.reshape(4, 4 * n, 2 * BLOCK), "x", rel_xy)
    mixed = jnp.moveaxis(mixed.reshape(2, 2, n, 2 * BLOCK), 1, 0)
    mixed = halves(mixed.reshape(2, 2 * n, 2 * BLOCK), "h", rel_h).astype(BF)
    own = mixed[:, :BLOCK].reshape(2, n, BLOCK)
    own = by_pair(own[0], own[1], ll)
    other = swap(mixed[:, BLOCK:], "c").reshape(2, n, BLOCK)
    other = by_pair(other[0], other[1], ll)
    mixed_out = by_pair(own, other, c).reshape(rows, BLOCK)

    return (mixed_out, gradient, jnp.stack(self_list), jnp.stack(cross_list))


def solution(mesh):
    finer = Mesh(mesh.devices.reshape(2, 4, 4, 2, 2, 2), (*DP, *MP))
    in_specs = (
        P(DP, MP),
        P(MP, DP),
        P(MP, DP),
        P(DP, MP),
        P(None, MP, None),
        P(None, MP, None),
        P(DP, MP),
    )
    out_specs = (P(DP, MP), P(DP, MP), P(None, MP, None), P(None, MP, None))
    return jax.shard_map(
        per_device, mesh=finer, in_specs=in_specs, out_specs=out_specs, check_vma=False
    )
```

```python
import functools

import jax
import jax.numpy as jnp
from jax import lax
from jax.experimental import pallas as pl
from jax.experimental.pallas import tpu as pltpu
from jax.sharding import Mesh
from jax.sharding import PartitionSpec as P

BLOCK = 256
SECTIONS = 5
TILE = 256
DP = ("h", "x")
MP = ("y", "lh", "ll", "c")
BF = jnp.bfloat16
F32 = jnp.float32
PARTNER = (("c", 1), ("ll", 1), ("lh", 1), ("y", 1), ("y", 2))
BATCHES = ((4, 3, 2), (1, 0))


def swap(value, axis, bits=1):
    count = lax.axis_size(axis)
    return lax.ppermute(value, axis, [(i, i ^ bits) for i in range(count)])


def pick(value, index, dim=0):
    return lax.dynamic_index_in_dim(value, index, dim, keepdims=False)


def dot(a, b):
    return jnp.dot(a, b, preferred_element_type=F32)


def dot_t(a, b):
    return lax.dot_general(a, b, (((1,), (1,)), ((), ())), preferred_element_type=F32)


def t_dot(a, b):
    return lax.dot_general(a, b, (((0,), (0,)), ((), ())), preferred_element_type=F32)


def f32(v):
    return v.astype(F32)


def tie(*values):
    return lax.optimization_barrier(values)


def gather4(value, axis):
    return [value] + [swap(value, axis, k) for k in (1, 2, 3)]


def scatter4(parts, axis):
    total = f32(parts[0])
    for k in (1, 2, 3):
        total = total + f32(swap(parts[k], axis, k))
    return total


def halves(parts, axis, mine):
    other = swap(pick(parts, 1 - mine).astype(BF), axis)
    return pick(parts, mine) + f32(other)


def by_pair(own, other, index, dim=0):
    return jnp.stack(
        [jnp.where(index == 0, own, other), jnp.where(index == 0, other, own)], axis=dim
    )


def expand_kernel(nb, groups, transposed, order_ref, *refs):
    xs = refs[:4]
    ws = refs[4 : 4 + groups * nb]
    outs = refs[4 + groups * nb : 8 + groups * nb]
    held = refs[-1]
    rows = xs[0].shape[0]
    subs, _, sub_rows, _ = outs[0].shape

    @pl.when(pl.program_id(0) == 0)
    def _():
        for k in range(4):
            at = pl.multiple_of((order_ref[0] ^ k) * rows, rows)
            held[pl.ds(at, rows), :] = xs[k][...]

    for g in range(groups):
        total = None
        for i in range(nb):
            left = held[:, i * BLOCK : (i + 1) * BLOCK]
            right = ws[g * nb + i][...]
            part = dot_t(left, right) if transposed else dot(left, right)
            total = part if total is None else total + part
        total = total.astype(BF)
        for j in range(4):
            for s in range(subs):
                at = j * rows + s * sub_rows
                outs[j][s, g] = total[at : at + sub_rows]


def expand(order, xs, weights, groups, subs, transposed):
    nb = len(weights) // groups
    rows = xs[0].shape[0]
    ff = weights[0].shape[0 if transposed else 1]
    piece = (subs, groups, rows // subs)
    w_spec = (
        pl.BlockSpec((TILE, BLOCK), lambda t: (t, 0))
        if transposed
        else pl.BlockSpec((BLOCK, TILE), lambda t: (0, t))
    )
    return pl.pallas_call(
        functools.partial(expand_kernel, nb, groups, transposed),
        grid=(ff // TILE,),
        in_specs=[pl.BlockSpec(memory_space=pltpu.SMEM)]
        + [pl.BlockSpec(xs[0].shape, lambda t: (0, 0))] * 4
        + [w_spec] * len(weights),
        out_specs=[pl.BlockSpec((*piece, TILE), lambda t: (0, 0, 0, t))] * 4,
        out_shape=[jax.ShapeDtypeStruct((*piece, ff), BF)] * 4,
        scratch_shapes=[pltpu.VMEM((4 * rows, nb * BLOCK), BF)],
        cost_estimate=pl.CostEstimate(
            flops=8 * rows * nb * BLOCK * groups * ff,
            bytes_accessed=2 * BLOCK * ff * len(weights) + 8 * rows * groups * ff,
            transcendentals=0,
        ),
    )(order, *xs, *weights)


def contract_kernel(nb, groups, transposed, order_ref, *refs):
    ys = refs[:4]
    ws = refs[4 : 4 + groups * nb]
    outs = refs[4 + groups * nb : 8 + groups * nb]
    total = refs[-1]
    rows = outs[0].shape[0]
    subs = ys[0].shape[0]
    step = pl.program_id(0)
    lefts = [
        jnp.concatenate([ys[j][s, g] for j in range(4) for s in range(subs)], axis=0)
        for g in range(groups)
    ]

    def product(i):
        out = None
        for g in range(groups):
            right = ws[g * nb + i][...]
            part = dot_t(lefts[g], right) if transposed else dot(lefts[g], right)
            out = part if out is None else out + part
        return out

    @pl.when(step == 0)
    def _():
        for i in range(nb):
            total[:, i * BLOCK : (i + 1) * BLOCK] = product(i)

    @pl.when(step > 0)
    def _():
        for i in range(nb):
            total[:, i * BLOCK : (i + 1) * BLOCK] += product(i)

    @pl.when(step == pl.num_programs(0) - 1)
    def _():
        for k in range(4):
            at = pl.multiple_of((order_ref[0] ^ k) * rows, rows)
            outs[k][...] = total[pl.ds(at, rows), :].astype(BF)


def contract(order, ys, weights, groups, transposed):
    nb = len(weights) // groups
    subs, _, sub_rows, ff = ys[0].shape
    rows = subs * sub_rows
    w_spec = (
        pl.BlockSpec((BLOCK, TILE), lambda t: (0, t))
        if transposed
        else pl.BlockSpec((TILE, BLOCK), lambda t: (t, 0))
    )
    return pl.pallas_call(
        functools.partial(contract_kernel, nb, groups, transposed),
        grid=(ff // TILE,),
        in_specs=[pl.BlockSpec(memory_space=pltpu.SMEM)]
        + [pl.BlockSpec((subs, groups, sub_rows, TILE), lambda t: (0, 0, 0, t))] * 4
        + [w_spec] * len(weights),
        out_specs=[pl.BlockSpec((rows, nb * BLOCK), lambda t: (0, 0))] * 4,
        out_shape=[jax.ShapeDtypeStruct((rows, nb * BLOCK), BF)] * 4,
        scratch_shapes=[pltpu.VMEM((4 * rows, nb * BLOCK), F32)],
        cost_estimate=pl.CostEstimate(
            flops=8 * rows * nb * BLOCK * groups * ff,
            bytes_accessed=2 * BLOCK * ff * len(weights) + 8 * rows * groups * ff,
            transcendentals=0,
        ),
    )(order, *ys, *weights)


def per_device(tokens, gate_weight, up_weight, down_weight, factor_self, factor_cross, cotangent):
    h, x, y, lh, ll, c = (lax.axis_index(a) for a in (*DP, *MP))
    order = (x ^ y).astype(jnp.int32).reshape(1)
    rows = tokens.shape[0]
    n = rows // 4
    ff = gate_weight.shape[1]

    both = jnp.stack([tokens, cotangent])
    both = by_pair(both, swap(both, "h"), h, 1)
    current = both[0].reshape(2 * rows, BLOCK)

    gate_far = swap(gate_weight, "ll")
    gate_near = swap(gate_weight, "c")
    up_near = swap(up_weight, "c")
    down_near = swap(down_weight, "c")

    halved = both[1].reshape(2, 2, 2 * n, BLOCK)
    cot = jnp.concatenate([pick(halved, c, 1), swap(pick(halved, 1 - c, 1), "c")], axis=2)
    cot = cot.reshape(4 * n, 2 * BLOCK)

    inputs = []
    partners = []
    for degree in range(SECTIONS):
        axis, bits = PARTNER[degree]
        partner = swap(current, axis, bits)
        if degree == 1:
            partner, cot, up_weight = tie(partner, cot, up_weight)
            cots = gather4(cot, "x")
            up_far = swap(up_weight, "ll")
        if degree == 3:
            partner, *cots = tie(partner, *cots)
            terms = expand(order, cots, [down_weight, down_near], 1, 1, True)
        inputs.append(current)
        partners.append(partner)
        result = dot(current, factor_self[degree]) + dot(partner, factor_cross[degree])
        current = result.astype(BF)

    current, *terms = tie(current, *terms)
    hid = scatter4(terms, "y").reshape(2, 2, n, ff)

    quarters = current.reshape(2, 2, 2, n, BLOCK)

    def quarter(dc, dl):
        return pick(pick(quarters, c ^ dc, 1), ll ^ dl, 1).reshape(2 * n, BLOCK)

    mine = jnp.concatenate(
        [
            quarter(0, 0),
            swap(quarter(1, 0), "c"),
            swap(quarter(0, 1), "ll"),
            swap(quarter(1, 1), ("ll", "c"), 3),
        ],
        axis=1,
    )
    mine, gate_far, up_far = tie(mine, gate_far, up_far)
    gates = [gate_weight, gate_near, gate_far, swap(gate_far, "c")]
    ups = [up_weight, up_near, up_far, swap(up_far, "c")]
    sums = expand(order, gather4(mine, "x"), gates + ups, 2, 2, False)

    hid = halves(hid, "lh", lh)
    hidden_grad = halves(hid, "ll", ll)
    sums = halves(scatter4(sums, "y"), "lh", lh)
    gate_sum = sums[0]
    up_sum = sums[1]

    logistic = jax.nn.sigmoid(gate_sum)
    hidden = (gate_sum * logistic * up_sum).astype(BF)
    gate_grad = hidden_grad * up_sum * logistic * (1.0 + gate_sum * (1.0 - logistic))
    up_grad = hidden_grad * gate_sum * logistic
    grads = jnp.stack([gate_grad.astype(BF), up_grad.astype(BF)])

    grads_far, hidden = tie(swap(grads, "lh"), hidden)
    grads = gather4(by_pair(grads, grads_far, lh), "y")
    hidden = by_pair(hidden, swap(hidden, "lh"), lh)
    hidden = by_pair(hidden, swap(hidden, "ll"), ll).reshape(4, 1, n, ff)
    hidden, *grads = tie(hidden, *grads)
    hiddens = gather4(hidden, "y")
    terms = contract(order, grads, gates + ups, 2, True)

    total = scatter4(terms, "x").astype(BF)
    total = (f32(total) + f32(swap(total, "h"))).astype(BF)
    blocks = [total[:, i * BLOCK : (i + 1) * BLOCK].reshape(2, n, BLOCK) for i in range(4)]
    near = by_pair(blocks[0], swap(blocks[2], "ll"), ll, 1)
    far = by_pair(swap(blocks[1], "c"), swap(blocks[3], ("ll", "c"), 3), ll, 1)
    gradient = by_pair(near, far, c, 1).reshape(2 * rows, BLOCK)

    gradient, *hiddens = tie(gradient, *hiddens)
    mixed = contract(order, hiddens, [down_weight, down_near], 1, False)

    def summed(batch):
        parts = jnp.stack(batch).astype(BF)
        count = parts.shape[0]
        parts = parts.reshape(count, 4, BLOCK // 4, BLOCK)
        part = scatter4([pick(parts, x ^ k, 1) for k in range(4)], "x").astype(BF)
        whole = jnp.stack(gather4(part, "x"))
        whole = jnp.stack([pick(whole, x ^ k) for k in range(4)], axis=1)
        return f32(whole).reshape(count, BLOCK, BLOCK)

    self_list = [None] * SECTIONS
    cross_list = [None] * SECTIONS
    batch = []
    for degree in reversed(range(SECTIONS)):
        axis, bits = PARTNER[degree]
        carried = dot_t(gradient, factor_cross[degree]).astype(BF)
        returned = swap(carried, axis, bits)
        batch += [t_dot(inputs[degree], gradient), t_dot(partners[degree], gradient)]
        for members in BATCHES:
            if degree == members[-1]:
                out = summed(batch)
                for i, d in enumerate(members):
                    self_list[d] = out[2 * i]
                    cross_list[d] = out[2 * i + 1]
                batch = []
        if degree == 4:
            returned, *mixed = tie(returned, *mixed)
            mixed = scatter4(mixed, "x")
        if degree == 2:
            returned, mixed = tie(returned, mixed)
        direct = dot_t(gradient, factor_self[degree])
        gradient = (direct + f32(returned)).astype(BF)
    input_grad = pick(gradient.reshape(2, rows, BLOCK), h)

    mixed = jnp.moveaxis(mixed.reshape(2, 2, n, 2 * BLOCK), 1, 0)
    mixed = halves(mixed, "h", h).astype(BF)
    other = swap(mixed[:, :, BLOCK:], "c")
    mixed_out = by_pair(mixed[:, :, :BLOCK], other, c).reshape(rows, BLOCK)

    return (mixed_out, input_grad, jnp.stack(self_list), jnp.stack(cross_list))


def solution(mesh):
    finer = Mesh(mesh.devices.reshape(2, 4, 4, 2, 2, 2), (*DP, *MP))
    in_specs = (
        P(DP, MP),
        P(MP, DP),
        P(MP, DP),
        P(DP, MP),
        P(None, MP, None),
        P(None, MP, None),
        P(DP, MP),
    )
    out_specs = (P(DP, MP), P(DP, MP), P(None, MP, None), P(None, MP, None))
    return jax.shard_map(
        per_device, mesh=finer, in_specs=in_specs, out_specs=out_specs, check_vma=False
    )
```

```python
import functools

import jax
import jax.numpy as jnp
from jax import lax
from jax.experimental import pallas as pl
from jax.experimental.pallas import tpu as pltpu
from jax.sharding import Mesh
from jax.sharding import PartitionSpec as P


BLOCK = 256
SECTIONS = 5
TILE = 256
DP = ("h", "x")
MP = ("y", "lh", "ll", "c")
BF = jnp.bfloat16
F32 = jnp.float32
PARTNER = (("c", 1), ("ll", 1), ("lh", 1), ("y", 1), ("y", 2))
BATCHES = ((4, 3, 2), (1, 0))


def swap(value, axis, bits=1):
    count = lax.axis_size(axis)
    return lax.ppermute(value, axis, [(i, i ^ bits) for i in range(count)])


def pick(value, index, dim=0):
    return lax.dynamic_index_in_dim(value, index, dim, keepdims=False)


def dot(a, b):
    return jnp.dot(a, b, preferred_element_type=F32)


def dot_t(a, b):
    return lax.dot_general(a, b, (((1,), (1,)), ((), ())), preferred_element_type=F32)


def t_dot(a, b):
    return lax.dot_general(a, b, (((0,), (0,)), ((), ())), preferred_element_type=F32)


def f32(v):
    return v.astype(F32)


def tie(*values):
    return lax.optimization_barrier(values)


def gather4(value, axis):
    return [value] + [swap(value, axis, k) for k in (1, 2, 3)]


def scatter4(parts, axis):
    total = f32(parts[0])
    for k in (1, 2, 3):
        total = total + f32(swap(parts[k], axis, k))
    return total


def halves(parts, axis, mine):
    other = swap(pick(parts, 1 - mine).astype(BF), axis)
    return pick(parts, mine) + f32(other)


def by_pair(own, other, index, dim=0):
    return jnp.stack(
        [jnp.where(index == 0, own, other), jnp.where(index == 0, other, own)], axis=dim
    )


VMEM = pl.BlockSpec(memory_space=pltpu.VMEM)
SMEM = pl.BlockSpec(memory_space=pltpu.SMEM)


def local_call(kernel, operands, out_shape, scratch, flops):
    moved = sum(v.size * v.dtype.itemsize for v in (*operands[1:], *out_shape))
    return pl.pallas_call(
        kernel,
        in_specs=[SMEM] + [VMEM] * (len(operands) - 1),
        out_specs=[VMEM] * len(out_shape),
        out_shape=out_shape,
        scratch_shapes=scratch,
        cost_estimate=pl.CostEstimate(flops=flops, bytes_accessed=moved, transcendentals=0),
        compiler_params=pltpu.CompilerParams(vmem_limit_bytes=60 * 1024 * 1024),
    )(*operands)


def taken(refs, counts):
    out = []
    for count in counts:
        out.append(refs[:count])
        refs = refs[count:]
    return out


def block_of(refs, index):
    parts = [r[index] for r in refs]
    return parts[0] if len(parts) == 1 else jnp.concatenate(parts, axis=0)


def expand_kernel(layout, groups, transposed, order_ref, *refs):
    xs, flat, outs, (held,) = taken(refs, (4, sum(layout), 4, 1))
    ws = taken(flat, layout)
    nb = len(ws) // groups
    rows = xs[0].shape[0]
    subs, _, sub_rows, ff = outs[0].shape
    for k in range(4):
        at = pl.multiple_of((order_ref[0] ^ k) * rows, rows)
        held[pl.ds(at, rows), :] = xs[k][...]

    @pl.loop(0, ff // TILE)
    def _(t):
        tile = pl.ds(pl.multiple_of(t * TILE, TILE), TILE)
        index = (tile, slice(None)) if transposed else (slice(None), tile)
        for g in range(groups):
            total = None
            for i in range(nb):
                left = held[:, i * BLOCK : (i + 1) * BLOCK]
                right = block_of(ws[g * nb + i], index)
                part = dot_t(left, right) if transposed else dot(left, right)
                total = part if total is None else total + part
            total = total.astype(BF)
            for j in range(4):
                for s in range(subs):
                    at = j * rows + s * sub_rows
                    outs[j][s, g, :, tile] = total[at : at + sub_rows]


def expand(order, xs, weights, groups, subs, transposed):
    layout = tuple(len(w) for w in weights)
    nb = len(weights) // groups
    rows = xs[0].shape[0]
    ff = weights[0][0].shape[0 if transposed else 1]
    return local_call(
        functools.partial(expand_kernel, layout, groups, transposed),
        [order, *xs, *(v for w in weights for v in w)],
        [jax.ShapeDtypeStruct((subs, groups, rows // subs, ff), BF)] * 4,
        [pltpu.VMEM((4 * rows, nb * BLOCK), BF)],
        8 * rows * nb * BLOCK * groups * ff,
    )


def contract_kernel(layout, groups, transposed, order_ref, *refs):
    ys, flat, outs, (total,) = taken(refs, (4, sum(layout), 4, 1))
    ws = taken(flat, layout)
    nb = len(ws) // groups
    rows = outs[0].shape[0]
    subs, _, _, ff = ys[0].shape
    total[...] = jnp.zeros_like(total)

    @pl.loop(0, ff // TILE)
    def _(t):
        tile = pl.ds(pl.multiple_of(t * TILE, TILE), TILE)
        index = (slice(None), tile) if transposed else (tile, slice(None))
        lefts = [
            jnp.concatenate(
                [ys[j][s, g, :, tile] for j in range(4) for s in range(subs)], axis=0
            )
            for g in range(groups)
        ]
        for i in range(nb):
            out = None
            for g in range(groups):
                right = block_of(ws[g * nb + i], index)
                part = dot_t(lefts[g], right) if transposed else dot(lefts[g], right)
                out = part if out is None else out + part
            total[:, i * BLOCK : (i + 1) * BLOCK] += out

    for k in range(4):
        at = pl.multiple_of((order_ref[0] ^ k) * rows, rows)
        outs[k][...] = total[pl.ds(at, rows), :].astype(BF)


def contract(order, ys, weights, groups, transposed):
    layout = tuple(len(w) for w in weights)
    nb = len(weights) // groups
    subs, _, sub_rows, ff = ys[0].shape
    rows = subs * sub_rows
    return local_call(
        functools.partial(contract_kernel, layout, groups, transposed),
        [order, *ys, *(v for w in weights for v in w)],
        [jax.ShapeDtypeStruct((rows, nb * BLOCK), BF)] * 4,
        [pltpu.VMEM((4 * rows, nb * BLOCK), F32)],
        8 * rows * nb * BLOCK * groups * ff,
    )


def factor_kernel(count, place_ref, *refs):
    lefts, rights, outs, (held,) = taken(refs, (2 * count, count, 4, 1))
    for i in range(2 * count):
        held[i] = t_dot(lefts[i][...], rights[i // 2][...]).astype(BF)
    part = BLOCK // 4
    for k in range(4):
        at = pl.multiple_of((place_ref[0] ^ k) * part, part)
        outs[k][...] = held[:, pl.ds(at, part), :]


def factor_parts(place, lefts, rights):
    count = len(rights)
    return local_call(
        functools.partial(factor_kernel, count),
        [place, *lefts, *rights],
        [jax.ShapeDtypeStruct((2 * count, BLOCK // 4, BLOCK), BF)] * 4,
        [pltpu.VMEM((2 * count, BLOCK, BLOCK), BF)],
        4 * count * lefts[0].shape[0] * BLOCK * BLOCK,
    )


def place_kernel(place_ref, *refs):
    part = BLOCK // 4
    *pieces, self_ref, cross_ref = refs
    for b, members in enumerate(BATCHES):
        for k in range(4):
            at = pl.multiple_of((place_ref[0] ^ k) * part, part)
            for i, degree in enumerate(members):
                self_ref[degree, pl.ds(at, part), :] = f32(pieces[4 * b + k][2 * i])
                cross_ref[degree, pl.ds(at, part), :] = f32(pieces[4 * b + k][2 * i + 1])


def body(tokens, gate_weight, up_weight, down_weight, factor_self, factor_cross, cotangent):
    h, x, y, lh, ll, c = (lax.axis_index(a) for a in (*DP, *MP))
    order = (x ^ y).astype(jnp.int32).reshape(1)
    place = x.astype(jnp.int32).reshape(1)
    rows = tokens.shape[0]
    n = rows // 4
    ff = gate_weight.shape[1]

    half = BLOCK // 2
    gate_far = [swap(gate_weight[:half], "ll")]
    gate_near = swap(gate_weight, "c")
    up_near = swap(up_weight, "c")
    down_near = swap(down_weight, "c")
    gate_far.append(swap(gate_weight[half:], "ll"))
    up_far = [swap(up_weight[:half], "ll"), swap(up_weight[half:], "ll")]

    both = jnp.stack([tokens, cotangent])
    both = by_pair(both, swap(both, "h"), h, 1)
    current = both[0].reshape(2 * rows, BLOCK)

    halved = both[1].reshape(2, 2, 2 * n, BLOCK)
    cot = jnp.concatenate([pick(halved, c, 1), swap(pick(halved, 1 - c, 1), "c")], axis=2)
    cots = gather4(cot.reshape(4 * n, 2 * BLOCK), "x")
    terms = expand(order, cots, [[down_weight], [down_near]], 1, 1, True)

    inputs = []
    partners = []
    for degree in range(SECTIONS):
        axis, bits = PARTNER[degree]
        partner = swap(current, axis, bits)
        inputs.append(current)
        partners.append(partner)
        result = dot(current, factor_self[degree]) + dot(partner, factor_cross[degree])
        current = result.astype(BF)

    quarters = current.reshape(2, 2, 2, n, BLOCK)

    def quarter(dc, dl):
        return pick(pick(quarters, c ^ dc, 1), ll ^ dl, 1).reshape(2 * n, BLOCK)

    mine = jnp.concatenate(
        [
            quarter(0, 0),
            swap(quarter(1, 0), "c"),
            swap(quarter(0, 1), "ll"),
            swap(quarter(1, 1), ("ll", "c"), 3),
        ],
        axis=1,
    )
    mine, *far = tie(mine, *gate_far, *up_far)
    rotated = gather4(mine, "x")
    cross = [swap(v, "c") for v in far]
    gates = [[gate_weight], [gate_near], far[:2], cross[:2]]
    ups = [[up_weight], [up_near], far[2:], cross[2:]]
    sums = expand(order, rotated, gates + ups, 2, 2, False)

    hid = scatter4(terms, "y").reshape(2, 2, n, ff)
    hid = halves(hid, "lh", lh)
    hidden_grad = halves(hid, "ll", ll)
    sums = halves(scatter4(sums, "y"), "lh", lh)
    gate_sum = sums[0]
    up_sum = sums[1]

    logistic = jax.nn.sigmoid(gate_sum)
    hidden = (gate_sum * logistic * up_sum).astype(BF)
    gate_grad = hidden_grad * up_sum * logistic * (1.0 + gate_sum * (1.0 - logistic))
    up_grad = hidden_grad * gate_sum * logistic
    grads = jnp.stack([gate_grad.astype(BF), up_grad.astype(BF)])

    grads = by_pair(grads, swap(grads, "lh"), lh)
    grads = gather4(grads, "y")
    hidden_far, grads[1] = tie(swap(hidden, "lh"), grads[1])
    hidden = by_pair(hidden, hidden_far, lh)
    hidden = by_pair(hidden, swap(hidden, "ll"), ll).reshape(4, 1, n, ff)
    hiddens = gather4(hidden, "y")
    terms = contract(order, grads, gates + ups, 2, True)

    total = scatter4(terms, "x").astype(BF)
    total = (f32(total) + f32(swap(total, "h"))).astype(BF)
    blocks = [total[:, i * BLOCK : (i + 1) * BLOCK].reshape(2, n, BLOCK) for i in range(4)]
    near = by_pair(blocks[0], swap(blocks[2], "ll"), ll, 1)
    far = by_pair(swap(blocks[1], "c"), swap(blocks[3], ("ll", "c"), 3), ll, 1)
    gradient = by_pair(near, far, c, 1).reshape(2 * rows, BLOCK)

    mixed = contract(order, hiddens, [[down_weight], [down_near]], 1, False)
    mixed = scatter4(mixed, "x")
    mixed = jnp.moveaxis(mixed.reshape(2, 2, n, 2 * BLOCK), 1, 0)
    mixed = halves(mixed, "h", h).astype(BF)
    other = swap(mixed[:, :, BLOCK:], "c")
    mixed_out = by_pair(mixed[:, :, :BLOCK], other, c).reshape(rows, BLOCK)

    ws = [None] * SECTIONS
    for degree in reversed(range(SECTIONS)):
        axis, bits = PARTNER[degree]
        ws[degree] = gradient
        carried = dot_t(gradient, factor_cross[degree]).astype(BF)
        returned = swap(carried, axis, bits)
        direct = dot_t(gradient, factor_self[degree])
        gradient = (direct + f32(returned)).astype(BF)
    input_grad = pick(gradient.reshape(2, rows, BLOCK), h)

    pieces = []
    for members in BATCHES:
        lefts = [v for d in members for v in (inputs[d], partners[d])]
        parts = factor_parts(place, lefts, [ws[d] for d in members])
        part = scatter4(parts, "x").astype(BF)
        pieces += gather4(part, "x")
    out = jax.ShapeDtypeStruct(factor_self.shape, F32)
    self_grad, cross_grad = local_call(place_kernel, [place, *pieces], [out, out], [], 0)

    return (mixed_out, input_grad, self_grad, cross_grad)


def solution(mesh):
    finer = Mesh(mesh.devices.reshape(2, 4, 4, 2, 2, 2), (*DP, *MP))
    in_specs = (
        P(DP, MP),
        P(MP, DP),
        P(MP, DP),
        P(DP, MP),
        P(None, MP, None),
        P(None, MP, None),
        P(DP, MP),
    )
    out_specs = (P(DP, MP), P(DP, MP), P(None, MP, None), P(None, MP, None))
    return jax.shard_map(body, mesh=finer, in_specs=in_specs, out_specs=out_specs, check_vma=False)
```

```python
import functools
import math

import jax
import jax.numpy as jnp
from jax import lax
from jax.experimental import pallas as pl
from jax.experimental.pallas import tpu as pltpu
from jax.sharding import Mesh
from jax.sharding import PartitionSpec as P


BLOCK = 256
SECTIONS = 5
TILE = 256
GRANT = 4 * 1024 * 1024
DP = ("h", "x")
MP = ("y", "lh", "ll", "c")
BF = jnp.bfloat16
F32 = jnp.float32
PARTNER = (("c", 1), ("ll", 1), ("lh", 1), ("y", 1), ("y", 2))
BATCHES = ((4, 3, 2), (1, 0))


def swap(value, axis, bits=1):
    count = lax.axis_size(axis)
    return lax.ppermute(value, axis, [(i, i ^ bits) for i in range(count)])


def pick(value, index, dim=0):
    return lax.dynamic_index_in_dim(value, index, dim, keepdims=False)


def dot(a, b):
    return jnp.dot(a, b, preferred_element_type=F32)


def dot_t(a, b):
    return lax.dot_general(a, b, (((1,), (1,)), ((), ())), preferred_element_type=F32)


def t_dot(a, b):
    return lax.dot_general(a, b, (((0,), (0,)), ((), ())), preferred_element_type=F32)


def f32(v):
    return v.astype(F32)


def tie(*values):
    return lax.optimization_barrier(values)


def gather4(value, axis):
    return [value] + [swap(value, axis, k) for k in (1, 2, 3)]


def sent4(parts, axis):
    return [parts[0]] + [swap(parts[k], axis, k) for k in (1, 2, 3)]


def summed(parts):
    total = f32(parts[0])
    for v in parts[1:]:
        total = total + f32(v)
    return total


def scatter4(parts, axis):
    return summed(sent4(parts, axis))


def halves(parts, axis, mine):
    other = swap(pick(parts, 1 - mine).astype(BF), axis)
    return pick(parts, mine) + f32(other)


def by_pair(own, other, index, dim=0):
    return jnp.stack(
        [jnp.where(index == 0, own, other), jnp.where(index == 0, other, own)], axis=dim
    )


VMEM = pl.BlockSpec(memory_space=pltpu.VMEM)
SMEM = pl.BlockSpec(memory_space=pltpu.SMEM)


def local_call(kernel, operands, out_shape, scratch, flops):
    moved = sum(v.size * v.dtype.itemsize for v in (*operands[1:], *out_shape))
    held = sum(math.prod(v.shape) * v.dtype.itemsize for v in scratch)
    grant = moved + held + GRANT
    out = pl.pallas_call(
        kernel,
        in_specs=[SMEM] + [VMEM] * (len(operands) - 1),
        out_specs=[VMEM] * len(out_shape),
        out_shape=out_shape,
        scratch_shapes=scratch,
        cost_estimate=pl.CostEstimate(flops=flops, bytes_accessed=moved, transcendentals=0),
        compiler_params=pltpu.CompilerParams(vmem_limit_bytes=grant),
    )(*operands)
    return list(out)


def taken(refs, counts):
    out = []
    for count in counts:
        out.append(refs[:count])
        refs = refs[count:]
    return out


def block_of(refs, index):
    parts = [r[index] for r in refs]
    return parts[0] if len(parts) == 1 else jnp.concatenate(parts, axis=0)


def expand_kernel(layout, groups, transposed, order_ref, *refs):
    xs, flat, outs, (held,) = taken(refs, (4, sum(layout), 4, 1))
    ws = taken(flat, layout)
    nb = len(ws) // groups
    rows = xs[0].shape[0]
    subs, _, sub_rows, ff = outs[0].shape
    for k in range(4):
        at = pl.multiple_of((order_ref[0] ^ k) * rows, rows)
        held[pl.ds(at, rows), :] = xs[k][...]

    @pl.loop(0, ff // TILE)
    def _(t):
        tile = pl.ds(pl.multiple_of(t * TILE, TILE), TILE)
        index = (tile, slice(None)) if transposed else (slice(None), tile)
        for g in range(groups):
            total = None
            for i in range(nb):
                left = held[:, i * BLOCK : (i + 1) * BLOCK]
                right = block_of(ws[g * nb + i], index)
                part = dot_t(left, right) if transposed else dot(left, right)
                total = part if total is None else total + part
            total = total.astype(BF)
            for j in range(4):
                for s in range(subs):
                    at = j * rows + s * sub_rows
                    outs[j][s, g, :, tile] = total[at : at + sub_rows]


def expand(order, xs, weights, groups, subs, transposed):
    layout = tuple(len(w) for w in weights)
    nb = len(weights) // groups
    rows = xs[0].shape[0]
    ff = weights[0][0].shape[0 if transposed else 1]
    return local_call(
        functools.partial(expand_kernel, layout, groups, transposed),
        [order, *xs, *(v for w in weights for v in w)],
        [jax.ShapeDtypeStruct((subs, groups, rows // subs, ff), BF)] * 4,
        [pltpu.VMEM((4 * rows, nb * BLOCK), BF)],
        8 * rows * nb * BLOCK * groups * ff,
    )


def contract_kernel(layout, groups, transposed, order_ref, *refs):
    ys, flat, outs, (total,) = taken(refs, (4, sum(layout), 4, 1))
    ws = taken(flat, layout)
    nb = len(ws) // groups
    rows = outs[0].shape[0]
    subs, _, _, ff = ys[0].shape
    total[...] = jnp.zeros_like(total)

    @pl.loop(0, ff // TILE)
    def _(t):
        tile = pl.ds(pl.multiple_of(t * TILE, TILE), TILE)
        index = (slice(None), tile) if transposed else (tile, slice(None))
        lefts = [
            jnp.concatenate(
                [ys[j][s, g, :, tile] for j in range(4) for s in range(subs)], axis=0
            )
            for g in range(groups)
        ]
        for i in range(nb):
            out = None
            for g in range(groups):
                right = block_of(ws[g * nb + i], index)
                part = dot_t(lefts[g], right) if transposed else dot(lefts[g], right)
                out = part if out is None else out + part
            total[:, i * BLOCK : (i + 1) * BLOCK] += out

    for k in range(4):
        at = pl.multiple_of((order_ref[0] ^ k) * rows, rows)
        outs[k][...] = total[pl.ds(at, rows), :].astype(BF)


def contract(order, ys, weights, groups, transposed):
    layout = tuple(len(w) for w in weights)
    nb = len(weights) // groups
    subs, _, sub_rows, ff = ys[0].shape
    rows = subs * sub_rows
    return local_call(
        functools.partial(contract_kernel, layout, groups, transposed),
        [order, *ys, *(v for w in weights for v in w)],
        [jax.ShapeDtypeStruct((rows, nb * BLOCK), BF)] * 4,
        [pltpu.VMEM((4 * rows, nb * BLOCK), F32)],
        8 * rows * nb * BLOCK * groups * ff,
    )


def factor_kernel(members, place_ref, near_ref, far_ref, *refs):
    rights, outs, (held,) = taken(refs, (len(members), 4, 1))
    first = place_ref[1] == 0
    for i, degree in enumerate(members):
        right = rights[i][...]
        for j in range(2):
            near = near_ref[degree + j * SECTIONS]
            far = far_ref[degree + j * SECTIONS]
            left = jnp.concatenate(
                [jnp.where(first, near, far), jnp.where(first, far, near)], axis=0
            )
            held[2 * i + j] = t_dot(left, right).astype(BF)
    part = BLOCK // 4
    for k in range(4):
        at = pl.multiple_of((place_ref[0] ^ k) * part, part)
        outs[k][...] = held[:, pl.ds(at, part), :]


def factor_parts(place, members, near, far, rights):
    count = 2 * len(members)
    return local_call(
        functools.partial(factor_kernel, members),
        [place, near, far, *rights],
        [jax.ShapeDtypeStruct((count, BLOCK // 4, BLOCK), BF)] * 4,
        [pltpu.VMEM((count, BLOCK, BLOCK), BF)],
        2 * count * rights[0].shape[0] * BLOCK * BLOCK,
    )


def stack_kernel(_, *refs):
    for i, ref in enumerate(refs[:-1]):
        refs[-1][i] = ref[...]


def place_kernel(place_ref, *refs):
    part = BLOCK // 4
    *pieces, self_ref, cross_ref = refs
    for b, members in enumerate(BATCHES):
        for k in range(4):
            at = pl.multiple_of((place_ref[0] ^ k) * part, part)
            for i, degree in enumerate(members):
                self_ref[degree, pl.ds(at, part), :] = f32(pieces[4 * b + k][2 * i])
                cross_ref[degree, pl.ds(at, part), :] = f32(pieces[4 * b + k][2 * i + 1])


def body(tokens, gate_weight, up_weight, down_weight, factor_self, factor_cross, cotangent):
    h, x, y, lh, ll, c = (lax.axis_index(a) for a in (*DP, *MP))
    order = (x ^ y).astype(jnp.int32).reshape(1)
    place = jnp.stack([x, h]).astype(jnp.int32)
    rows = tokens.shape[0]
    n = rows // 4
    ff = gate_weight.shape[1]

    half = BLOCK // 2
    gate_far = [swap(gate_weight[:half], "ll")]
    gate_near = swap(gate_weight, "c")
    up_near = swap(up_weight, "c")
    down_near = swap(down_weight, "c")
    gate_far.append(swap(gate_weight[half:], "ll"))
    up_far = [swap(up_weight[:half], "ll"), swap(up_weight[half:], "ll")]

    halved = cotangent.reshape(2, 2 * n, BLOCK)
    cot = jnp.concatenate([pick(halved, c), swap(pick(halved, 1 - c), "c")], axis=1)
    cot = by_pair(cot, swap(cot, "h"), h)
    cots = gather4(cot.reshape(4 * n, 2 * BLOCK), "x")
    terms = expand(order, cots, [[down_weight], [down_near]], 1, 1, True)

    current = tokens
    inputs = []
    partners = []
    for degree in range(SECTIONS):
        axis, bits = PARTNER[degree]
        partner = swap(current, axis, bits)
        inputs.append(current)
        partners.append(partner)
        result = dot(current, factor_self[degree]) + dot(partner, factor_cross[degree])
        current = result.astype(BF)

    quarters = current.reshape(2, 2, n, BLOCK)

    def quarter(dc, dl):
        return pick(pick(quarters, c ^ dc), ll ^ dl)

    mine = jnp.concatenate(
        [
            quarter(0, 0),
            swap(quarter(1, 0), "c"),
            swap(quarter(0, 1), "ll"),
            swap(quarter(1, 1), ("ll", "c"), 3),
        ],
        axis=1,
    )
    mine, *gate_far = tie(mine, *gate_far)
    mine = by_pair(mine, swap(mine, "h"), h).reshape(2 * n, 4 * BLOCK)
    rotated = gather4(mine, "x")
    rotated[2], *up_far = tie(rotated[2], *up_far)
    gate_cross = [swap(v, "c") for v in gate_far]
    up_cross = [swap(v, "c") for v in up_far]
    gates = [[gate_weight], [gate_near], gate_far, gate_cross]
    ups = [[up_weight], [up_near], up_far, up_cross]
    sums = expand(order, rotated, gates + ups, 2, 2, False)

    sums = sent4(sums, "y")
    sums[1], *terms = tie(sums[1], *sent4(terms, "y"))
    hid = summed(terms).reshape(2, 2, n, ff)
    hid = halves(hid, "lh", lh)
    hidden_grad = halves(hid, "ll", ll)
    sums = halves(summed(sums), "lh", lh)
    gate_sum = sums[0]
    up_sum = sums[1]

    logistic = jax.nn.sigmoid(gate_sum)
    hidden = (gate_sum * logistic * up_sum).astype(BF)
    gate_grad = hidden_grad * up_sum * logistic * (1.0 + gate_sum * (1.0 - logistic))
    up_grad = hidden_grad * gate_sum * logistic
    grads = jnp.stack([gate_grad.astype(BF), up_grad.astype(BF)])

    grads = by_pair(grads, swap(grads, "lh"), lh)
    grads = gather4(grads, "y")
    hidden_far, grads[1] = tie(swap(hidden, "lh"), grads[1])
    hidden = by_pair(hidden, hidden_far, lh)
    hidden = by_pair(hidden, swap(hidden, "ll"), ll).reshape(4, 1, n, ff)
    hiddens = gather4(hidden, "y")
    count = 2 * SECTIONS
    shape = jax.ShapeDtypeStruct((count, rows, BLOCK), BF)
    (saved,) = local_call(stack_kernel, [place, *inputs, *partners], [shape], [], 0)
    saved_far = swap(saved, "h")
    terms = contract(order, grads, gates + ups, 2, True)

    total = scatter4(terms, "x").astype(BF)
    total = (f32(total) + f32(swap(total, "h"))).astype(BF)
    blocks = [total[:, i * BLOCK : (i + 1) * BLOCK].reshape(2, n, BLOCK) for i in range(4)]
    near = by_pair(blocks[0], swap(blocks[2], "ll"), ll, 1)
    far = by_pair(swap(blocks[1], "c"), swap(blocks[3], ("ll", "c"), 3), ll, 1)
    gradient = by_pair(near, far, c, 1).reshape(2 * rows, BLOCK)

    mixed = contract(order, hiddens, [[down_weight], [down_near]], 1, False)
    mixed = sent4(mixed, "x")

    ws = [None] * SECTIONS
    for degree in reversed(range(SECTIONS)):
        axis, bits = PARTNER[degree]
        ws[degree] = gradient
        carried = dot_t(gradient, factor_cross[degree]).astype(BF)
        returned = swap(carried, axis, bits)
        if degree == 2:
            returned, *mixed = tie(returned, *mixed)
            mixed = summed(mixed).reshape(2, 2, n, 2 * BLOCK)
            mixed_far = swap(pick(mixed, 1 - h, 1).astype(BF), "h")
        direct = dot_t(gradient, factor_self[degree])
        gradient = (direct + f32(returned)).astype(BF)
    input_grad = pick(gradient.reshape(2, rows, BLOCK), h)

    early, late = [
        factor_parts(place, members, saved, saved_far, [ws[d] for d in members])
        for members in BATCHES
    ]
    early = sent4(early, "x")
    late[0], mixed_far, *early = tie(late[0], mixed_far, *early)
    late = summed(sent4(late, "x")).astype(BF)
    pieces = gather4(summed(early).astype(BF), "x") + gather4(late, "x")
    out = jax.ShapeDtypeStruct(factor_self.shape, F32)
    self_grad, cross_grad = local_call(place_kernel, [place, *pieces], [out, out], [], 0)

    mixed = (pick(mixed, h, 1) + f32(mixed_far)).astype(BF)
    other = swap(mixed[:, :, BLOCK:], "c")
    mixed_out = by_pair(mixed[:, :, :BLOCK], other, c).reshape(rows, BLOCK)

    return (mixed_out, input_grad, self_grad, cross_grad)


def solution(mesh):
    finer = Mesh(mesh.devices.reshape(2, 4, 4, 2, 2, 2), (*DP, *MP))
    in_specs = (
        P(DP, MP),
        P(MP, DP),
        P(MP, DP),
        P(DP, MP),
        P(None, MP, None),
        P(None, MP, None),
        P(DP, MP),
    )
    out_specs = (P(DP, MP), P(DP, MP), P(None, MP, None), P(None, MP, None))
    return jax.shard_map(body, mesh=finer, in_specs=in_specs, out_specs=out_specs, check_vma=False)
```

```python
import functools

import jax
import jax.numpy as jnp
from jax import lax
from jax.experimental import pallas as pl
from jax.experimental.pallas import tpu as pltpu
from jax.sharding import Mesh
from jax.sharding import PartitionSpec as P


BLOCK = 256
SECTIONS = 5
TILE = 256
GRANT = 60 * 1024 * 1024
PARTS = ((0, 3), (3, 7))
DP = ("h", "x")
MP = ("y", "lh", "ll", "c")
BF = jnp.bfloat16
F32 = jnp.float32
PARTNER = (("c", 1), ("ll", 1), ("lh", 1), ("y", 1), ("y", 2))
BATCHES = ((4, 3, 2), (1, 0))


def swap(value, axis, bits=1):
    count = lax.axis_size(axis)
    return lax.ppermute(value, axis, [(i, i ^ bits) for i in range(count)])


def pick(value, index, dim=0):
    return lax.dynamic_index_in_dim(value, index, dim, keepdims=False)


def dot(a, b):
    return jnp.dot(a, b, preferred_element_type=F32)


def dot_t(a, b):
    return lax.dot_general(a, b, (((1,), (1,)), ((), ())), preferred_element_type=F32)


def t_dot(a, b):
    return lax.dot_general(a, b, (((0,), (0,)), ((), ())), preferred_element_type=F32)


def f32(v):
    return v.astype(F32)


def tie(*values):
    return lax.optimization_barrier(values)


def gather4(value, axis):
    return [value] + [swap(value, axis, k) for k in (1, 2, 3)]


def sent4(parts, axis):
    return [parts[0]] + [swap(parts[k], axis, k) for k in (1, 2, 3)]


def summed(parts):
    total = f32(parts[0])
    for v in parts[1:]:
        total = total + f32(v)
    return total


def scatter4(parts, axis):
    return summed(sent4(parts, axis))


def halves(parts, axis, mine):
    other = swap(pick(parts, 1 - mine).astype(BF), axis)
    return pick(parts, mine) + f32(other)


def by_pair(own, other, index, dim=0):
    return jnp.stack(
        [jnp.where(index == 0, own, other), jnp.where(index == 0, other, own)], axis=dim
    )


VMEM = pl.BlockSpec(memory_space=pltpu.VMEM)
SMEM = pl.BlockSpec(memory_space=pltpu.SMEM)


def local_call(kernel, operands, out_shape, scratch, flops, fetched=0):
    if fetched:
        arrays = operands[-fetched:]
        scratch = [
            *scratch,
            *(pltpu.VMEM(v.shape, v.dtype) for v in arrays),
            pltpu.SemaphoreType.DMA((len(PARTS), fetched)),
        ]
    moved = sum(v.size * v.dtype.itemsize for v in (*operands[1:], *out_shape))
    out = pl.pallas_call(
        kernel,
        in_specs=[SMEM]
        + [VMEM] * (len(operands) - 1 - fetched)
        + [pl.BlockSpec(memory_space=pl.ANY)] * fetched,
        out_specs=[VMEM] * len(out_shape),
        out_shape=out_shape,
        scratch_shapes=scratch,
        cost_estimate=pl.CostEstimate(flops=flops, bytes_accessed=moved, transcendentals=0),
        compiler_params=pltpu.CompilerParams(vmem_limit_bytes=GRANT),
    )(*operands)
    return list(out)


def taken(refs, counts):
    out = []
    for count in counts:
        out.append(refs[:count])
        refs = refs[count:]
    return out


def block_of(refs, index):
    parts = [r[index] for r in refs]
    return parts[0] if len(parts) == 1 else jnp.concatenate(parts, axis=0)


def fetch(sources, targets, sems, across):
    copies = []
    for p, (low, high) in enumerate(PARTS):
        units = slice(low * TILE, high * TILE)
        index = (slice(None), units) if across else (units, slice(None))
        copies.append(
            [
                pltpu.make_async_copy(v.at[index], to.at[index], sems.at[p, i])
                for i, (v, to) in enumerate(zip(sources, targets))
            ]
        )
    for part in copies:
        for copy in part:
            copy.start()

    def arrived(p):
        for copy in copies[p]:
            copy.wait()

    return arrived


def expand_kernel(layout, groups, transposed, order_ref, *refs):
    count = sum(layout)
    xs, sources, outs, (held,), flat, (sems,) = taken(refs, (4, count, 4, 1, count, 1))
    arrived = fetch(sources, flat, sems, not transposed)
    ws = taken(flat, layout)
    nb = len(ws) // groups
    rows = xs[0].shape[0]
    subs, _, sub_rows, _ = outs[0].shape
    for k in range(4):
        at = pl.multiple_of((order_ref[0] ^ k) * rows, rows)
        held[pl.ds(at, rows), :] = xs[k][...]

    def step(t):
        tile = pl.ds(pl.multiple_of(t * TILE, TILE), TILE)
        index = (tile, slice(None)) if transposed else (slice(None), tile)
        for g in range(groups):
            total = None
            for i in range(nb):
                left = held[:, i * BLOCK : (i + 1) * BLOCK]
                right = block_of(ws[g * nb + i], index)
                part = dot_t(left, right) if transposed else dot(left, right)
                total = part if total is None else total + part
            total = total.astype(BF)
            for j in range(4):
                for s in range(subs):
                    at = j * rows + s * sub_rows
                    outs[j][s, g, :, tile] = total[at : at + sub_rows]

    for p, (low, high) in enumerate(PARTS):
        arrived(p)
        pl.loop(low, high)(step)


def expand(order, xs, weights, groups, subs, transposed):
    layout = tuple(len(w) for w in weights)
    nb = len(weights) // groups
    rows = xs[0].shape[0]
    ff = weights[0][0].shape[0 if transposed else 1]
    return local_call(
        functools.partial(expand_kernel, layout, groups, transposed),
        [order, *xs, *(v for w in weights for v in w)],
        [jax.ShapeDtypeStruct((subs, groups, rows // subs, ff), BF)] * 4,
        [pltpu.VMEM((4 * rows, nb * BLOCK), BF)],
        8 * rows * nb * BLOCK * groups * ff,
        sum(layout),
    )


def contract_kernel(layout, groups, transposed, order_ref, *refs):
    count = sum(layout)
    ys, sources, outs, (total,), flat, (sems,) = taken(refs, (4, count, 4, 1, count, 1))
    arrived = fetch(sources, flat, sems, transposed)
    ws = taken(flat, layout)
    nb = len(ws) // groups
    rows = outs[0].shape[0]
    subs, _, _, _ = ys[0].shape
    total[...] = jnp.zeros_like(total)

    def step(t):
        tile = pl.ds(pl.multiple_of(t * TILE, TILE), TILE)
        index = (slice(None), tile) if transposed else (tile, slice(None))
        lefts = [
            jnp.concatenate(
                [ys[j][s, g, :, tile] for j in range(4) for s in range(subs)], axis=0
            )
            for g in range(groups)
        ]
        for i in range(nb):
            out = None
            for g in range(groups):
                right = block_of(ws[g * nb + i], index)
                part = dot_t(lefts[g], right) if transposed else dot(lefts[g], right)
                out = part if out is None else out + part
            total[:, i * BLOCK : (i + 1) * BLOCK] += out

    for p, (low, high) in enumerate(PARTS):
        arrived(p)
        pl.loop(low, high)(step)

    for k in range(4):
        at = pl.multiple_of((order_ref[0] ^ k) * rows, rows)
        outs[k][...] = total[pl.ds(at, rows), :].astype(BF)


def contract(order, ys, weights, groups, transposed):
    layout = tuple(len(w) for w in weights)
    nb = len(weights) // groups
    subs, _, sub_rows, ff = ys[0].shape
    rows = subs * sub_rows
    return local_call(
        functools.partial(contract_kernel, layout, groups, transposed),
        [order, *ys, *(v for w in weights for v in w)],
        [jax.ShapeDtypeStruct((rows, nb * BLOCK), BF)] * 4,
        [pltpu.VMEM((4 * rows, nb * BLOCK), F32)],
        8 * rows * nb * BLOCK * groups * ff,
        sum(layout),
    )


def factor_kernel(members, place_ref, near_ref, far_ref, *refs):
    rights, outs, (held,) = taken(refs, (len(members), 4, 1))
    first = place_ref[1] == 0
    for i, degree in enumerate(members):
        right = rights[i][...]
        for j in range(2):
            near = near_ref[degree + j * SECTIONS]
            far = far_ref[degree + j * SECTIONS]
            left = jnp.concatenate(
                [jnp.where(first, near, far), jnp.where(first, far, near)], axis=0
            )
            held[2 * i + j] = t_dot(left, right).astype(BF)
    part = BLOCK // 4
    for k in range(4):
        at = pl.multiple_of((place_ref[0] ^ k) * part, part)
        outs[k][...] = held[:, pl.ds(at, part), :]


def factor_parts(place, members, near, far, rights):
    count = 2 * len(members)
    return local_call(
        functools.partial(factor_kernel, members),
        [place, near, far, *rights],
        [jax.ShapeDtypeStruct((count, BLOCK // 4, BLOCK), BF)] * 4,
        [pltpu.VMEM((count, BLOCK, BLOCK), BF)],
        2 * count * rights[0].shape[0] * BLOCK * BLOCK,
    )


def stack_kernel(_, *refs):
    for i, ref in enumerate(refs[:-1]):
        refs[-1][i] = ref[...]


def place_kernel(place_ref, *refs):
    part = BLOCK // 4
    *pieces, self_ref, cross_ref = refs
    for b, members in enumerate(BATCHES):
        for k in range(4):
            at = pl.multiple_of((place_ref[0] ^ k) * part, part)
            for i, degree in enumerate(members):
                self_ref[degree, pl.ds(at, part), :] = f32(pieces[4 * b + k][2 * i])
                cross_ref[degree, pl.ds(at, part), :] = f32(pieces[4 * b + k][2 * i + 1])


def body(tokens, gate_weight, up_weight, down_weight, factor_self, factor_cross, cotangent):
    h, x, y, lh, ll, c = (lax.axis_index(a) for a in (*DP, *MP))
    order = (x ^ y).astype(jnp.int32).reshape(1)
    place = jnp.stack([x, h]).astype(jnp.int32)
    rows = tokens.shape[0]
    n = rows // 4
    ff = gate_weight.shape[1]

    half = BLOCK // 2
    gate_far = [swap(gate_weight[:half], "ll")]
    gate_near = swap(gate_weight, "c")
    up_near = swap(up_weight, "c")
    down_near = swap(down_weight, "c")
    gate_far.append(swap(gate_weight[half:], "ll"))
    up_far = [swap(up_weight[:half], "ll"), swap(up_weight[half:], "ll")]

    halved = cotangent.reshape(2, 2 * n, BLOCK)
    cot = jnp.concatenate([pick(halved, c), swap(pick(halved, 1 - c), "c")], axis=1)
    cot = by_pair(cot, swap(cot, "h"), h)
    cots = gather4(cot.reshape(4 * n, 2 * BLOCK), "x")
    terms = expand(order, cots, [[down_weight], [down_near]], 1, 1, True)

    current = tokens
    inputs = []
    partners = []
    for degree in range(SECTIONS):
        axis, bits = PARTNER[degree]
        partner = swap(current, axis, bits)
        inputs.append(current)
        partners.append(partner)
        result = dot(current, factor_self[degree]) + dot(partner, factor_cross[degree])
        current = result.astype(BF)

    count = 2 * SECTIONS
    shape = jax.ShapeDtypeStruct((count, rows, BLOCK), BF)
    (saved,) = local_call(stack_kernel, [place, *inputs, *partners], [shape], [], 0)
    saved_far = swap(saved, "h")

    quarters = current.reshape(2, 2, n, BLOCK)

    def quarter(dc, dl):
        return pick(pick(quarters, c ^ dc), ll ^ dl)

    mine = jnp.concatenate(
        [
            quarter(0, 0),
            swap(quarter(1, 0), "c"),
            swap(quarter(0, 1), "ll"),
            swap(quarter(1, 1), ("ll", "c"), 3),
        ],
        axis=1,
    )
    mine, *gate_far = tie(mine, *gate_far)
    mine = by_pair(mine, swap(mine, "h"), h).reshape(2 * n, 4 * BLOCK)
    rotated = gather4(mine, "x")
    rotated[2], *up_far = tie(rotated[2], *up_far)
    gate_cross = [swap(v, "c") for v in gate_far]
    up_cross = [swap(v, "c") for v in up_far]
    gates = [[gate_weight], [gate_near], gate_far, gate_cross]
    ups = [[up_weight], [up_near], up_far, up_cross]
    sums = expand(order, rotated, gates + ups, 2, 2, False)

    sums = sent4(sums, "y")
    sums[1], *terms = tie(sums[1], *sent4(terms, "y"))
    hid = summed(terms).reshape(2, 2, n, ff)
    hid = halves(hid, "lh", lh)
    hidden_grad = halves(hid, "ll", ll)
    sums = halves(summed(sums), "lh", lh)
    gate_sum = sums[0]
    up_sum = sums[1]

    logistic = jax.nn.sigmoid(gate_sum)
    hidden = (gate_sum * logistic * up_sum).astype(BF)
    gate_grad = hidden_grad * up_sum * logistic * (1.0 + gate_sum * (1.0 - logistic))
    up_grad = hidden_grad * gate_sum * logistic
    grads = jnp.stack([gate_grad.astype(BF), up_grad.astype(BF)])

    grads = by_pair(grads, swap(grads, "lh"), lh)
    grads = gather4(grads, "y")
    hidden_far, grads[1] = tie(swap(hidden, "lh"), grads[1])
    hidden = by_pair(hidden, hidden_far, lh)
    hidden = by_pair(hidden, swap(hidden, "ll"), ll).reshape(4, 1, n, ff)
    hiddens = gather4(hidden, "y")
    terms = contract(order, grads, gates + ups, 2, True)

    total = scatter4(terms, "x").astype(BF)
    total = (f32(total) + f32(swap(total, "h"))).astype(BF)
    blocks = [total[:, i * BLOCK : (i + 1) * BLOCK].reshape(2, n, BLOCK) for i in range(4)]
    near = by_pair(blocks[0], swap(blocks[2], "ll"), ll, 1)
    far = by_pair(swap(blocks[1], "c"), swap(blocks[3], ("ll", "c"), 3), ll, 1)
    gradient = by_pair(near, far, c, 1).reshape(2 * rows, BLOCK)

    mixed = contract(order, hiddens, [[down_weight], [down_near]], 1, False)
    mixed = sent4(mixed, "x")

    ws = [None] * SECTIONS
    for degree in reversed(range(SECTIONS)):
        axis, bits = PARTNER[degree]
        ws[degree] = gradient
        carried = dot_t(gradient, factor_cross[degree]).astype(BF)
        returned = swap(carried, axis, bits)
        if degree == 2:
            returned, *mixed = tie(returned, *mixed)
            mixed = summed(mixed).reshape(2, 2, n, 2 * BLOCK)
            mixed_far = swap(pick(mixed, 1 - h, 1).astype(BF), "h")
        direct = dot_t(gradient, factor_self[degree])
        gradient = (direct + f32(returned)).astype(BF)
    input_grad = pick(gradient.reshape(2, rows, BLOCK), h)

    early, late = [
        factor_parts(place, members, saved, saved_far, [ws[d] for d in members])
        for members in BATCHES
    ]
    early = sent4(early, "x")
    late[0], mixed_far, *early = tie(late[0], mixed_far, *early)
    late = summed(sent4(late, "x")).astype(BF)
    pieces = gather4(summed(early).astype(BF), "x") + gather4(late, "x")
    out = jax.ShapeDtypeStruct(factor_self.shape, F32)
    self_grad, cross_grad = local_call(place_kernel, [place, *pieces], [out, out], [], 0)

    mixed = (pick(mixed, h, 1) + f32(mixed_far)).astype(BF)
    other = swap(mixed[:, :, BLOCK:], "c")
    mixed_out = by_pair(mixed[:, :, :BLOCK], other, c).reshape(rows, BLOCK)

    return (mixed_out, input_grad, self_grad, cross_grad)


def solution(mesh):
    finer = Mesh(mesh.devices.reshape(2, 4, 4, 2, 2, 2), (*DP, *MP))
    in_specs = (
        P(DP, MP),
        P(MP, DP),
        P(MP, DP),
        P(DP, MP),
        P(None, MP, None),
        P(None, MP, None),
        P(DP, MP),
    )
    out_specs = (P(DP, MP), P(DP, MP), P(None, MP, None), P(None, MP, None))
    return jax.shard_map(body, mesh=finer, in_specs=in_specs, out_specs=out_specs, check_vma=False)
```

```python
import functools

import jax
import jax.numpy as jnp
from jax import lax
from jax.experimental import pallas as pl
from jax.experimental.pallas import tpu as pltpu
from jax.sharding import Mesh
from jax.sharding import PartitionSpec as P


BLOCK = 256
SECTIONS = 5
TILE = 256
GRANT = 60 * 1024 * 1024
PARTS = ((0, 3), (3, 7))
DP = ("h", "x")
MP = ("y", "lh", "ll", "c")
BF = jnp.bfloat16
F32 = jnp.float32
PARTNER = (("c", 1), ("ll", 1), ("lh", 1), ("y", 1), ("y", 2))
BATCHES = ((4, 3, 2), (1, 0))


def swap(value, axis, bits=1):
    count = lax.axis_size(axis)
    return lax.ppermute(value, axis, [(i, i ^ bits) for i in range(count)])


def pick(value, index, dim=0):
    return lax.dynamic_index_in_dim(value, index, dim, keepdims=False)


def dot(a, b):
    return jnp.dot(a, b, preferred_element_type=F32)


def dot_t(a, b):
    return lax.dot_general(a, b, (((1,), (1,)), ((), ())), preferred_element_type=F32)


def t_dot(a, b):
    return lax.dot_general(a, b, (((0,), (0,)), ((), ())), preferred_element_type=F32)


def f32(v):
    return v.astype(F32)


def tie(*values):
    return lax.optimization_barrier(values)


def gather4(value, axis):
    return [value] + [swap(value, axis, k) for k in (1, 2, 3)]


def sent4(parts, axis):
    return [parts[0]] + [swap(parts[k], axis, k) for k in (1, 2, 3)]


def summed(parts):
    total = f32(parts[0])
    for v in parts[1:]:
        total = total + f32(v)
    return total


def scatter4(parts, axis):
    return summed(sent4(parts, axis))


def halves(parts, axis, mine):
    other = swap(pick(parts, 1 - mine).astype(BF), axis)
    return pick(parts, mine) + f32(other)


def by_pair(own, other, index, dim=0):
    return jnp.stack(
        [jnp.where(index == 0, own, other), jnp.where(index == 0, other, own)], axis=dim
    )


VMEM = pl.BlockSpec(memory_space=pltpu.VMEM)
SMEM = pl.BlockSpec(memory_space=pltpu.SMEM)


def local_call(kernel, operands, out_shape, scratch, flops, fetched=0):
    if fetched:
        arrays = operands[-fetched:]
        scratch = [
            *scratch,
            *(pltpu.VMEM(v.shape, v.dtype) for v in arrays),
            pltpu.SemaphoreType.DMA((len(PARTS), fetched)),
        ]
    moved = sum(v.size * v.dtype.itemsize for v in (*operands[1:], *out_shape))
    out = pl.pallas_call(
        kernel,
        in_specs=[SMEM]
        + [VMEM] * (len(operands) - 1 - fetched)
        + [pl.BlockSpec(memory_space=pl.ANY)] * fetched,
        out_specs=[VMEM] * len(out_shape),
        out_shape=out_shape,
        scratch_shapes=scratch,
        cost_estimate=pl.CostEstimate(flops=flops, bytes_accessed=moved, transcendentals=0),
        compiler_params=pltpu.CompilerParams(vmem_limit_bytes=GRANT),
    )(*operands)
    return list(out)


def taken(refs, counts):
    out = []
    for count in counts:
        out.append(refs[:count])
        refs = refs[count:]
    return out


def block_of(refs, index):
    parts = [r[index] for r in refs]
    return parts[0] if len(parts) == 1 else jnp.concatenate(parts, axis=0)


def fetch(sources, targets, sems, across):
    copies = []
    for p, (low, high) in enumerate(PARTS):
        units = slice(low * TILE, high * TILE)
        index = (slice(None), units) if across else (units, slice(None))
        copies.append(
            [
                pltpu.make_async_copy(v.at[index], to.at[index], sems.at[p, i])
                for i, (v, to) in enumerate(zip(sources, targets))
            ]
        )
    for part in copies:
        for copy in part:
            copy.start()

    def arrived(p):
        for copy in copies[p]:
            copy.wait()

    return arrived


def expand_kernel(layout, groups, transposed, order_ref, *refs):
    count = sum(layout)
    xs, sources, outs, (held,), flat, (sems,) = taken(refs, (4, count, 4, 1, count, 1))
    arrived = fetch(sources, flat, sems, not transposed)
    ws = taken(flat, layout)
    nb = len(ws) // groups
    rows = xs[0].shape[0]
    subs, _, sub_rows, _ = outs[0].shape
    for k in range(4):
        at = pl.multiple_of((order_ref[0] ^ k) * rows, rows)
        held[pl.ds(at, rows), :] = xs[k][...]

    def step(t):
        tile = pl.ds(pl.multiple_of(t * TILE, TILE), TILE)
        index = (tile, slice(None)) if transposed else (slice(None), tile)
        for g in range(groups):
            total = None
            for i in range(nb):
                left = held[:, i * BLOCK : (i + 1) * BLOCK]
                right = block_of(ws[g * nb + i], index)
                part = dot_t(left, right) if transposed else dot(left, right)
                total = part if total is None else total + part
            total = total.astype(BF)
            for j in range(4):
                for s in range(subs):
                    at = j * rows + s * sub_rows
                    outs[j][s, g, :, tile] = total[at : at + sub_rows]

    for p, (low, high) in enumerate(PARTS):
        arrived(p)
        pl.loop(low, high)(step)


def expand(order, xs, weights, groups, subs, transposed):
    layout = tuple(len(w) for w in weights)
    nb = len(weights) // groups
    rows = xs[0].shape[0]
    ff = weights[0][0].shape[0 if transposed else 1]
    return local_call(
        functools.partial(expand_kernel, layout, groups, transposed),
        [order, *xs, *(v for w in weights for v in w)],
        [jax.ShapeDtypeStruct((subs, groups, rows // subs, ff), BF)] * 4,
        [pltpu.VMEM((4 * rows, nb * BLOCK), BF)],
        8 * rows * nb * BLOCK * groups * ff,
        sum(layout),
    )


def contract_kernel(layout, groups, transposed, order_ref, *refs):
    count = sum(layout)
    ys, sources, outs, (total,), flat, (sems,) = taken(refs, (4, count, 4, 1, count, 1))
    arrived = fetch(sources, flat, sems, transposed)
    ws = taken(flat, layout)
    nb = len(ws) // groups
    rows = outs[0].shape[0]
    subs, _, _, _ = ys[0].shape
    total[...] = jnp.zeros_like(total)

    def step(t):
        tile = pl.ds(pl.multiple_of(t * TILE, TILE), TILE)
        index = (slice(None), tile) if transposed else (tile, slice(None))
        lefts = [
            jnp.concatenate(
                [ys[j][s, g, :, tile] for j in range(4) for s in range(subs)], axis=0
            )
            for g in range(groups)
        ]
        for i in range(nb):
            out = None
            for g in range(groups):
                right = block_of(ws[g * nb + i], index)
                part = dot_t(lefts[g], right) if transposed else dot(lefts[g], right)
                out = part if out is None else out + part
            total[:, i * BLOCK : (i + 1) * BLOCK] += out

    for p, (low, high) in enumerate(PARTS):
        arrived(p)
        pl.loop(low, high)(step)

    for k in range(4):
        at = pl.multiple_of((order_ref[0] ^ k) * rows, rows)
        outs[k][...] = total[pl.ds(at, rows), :].astype(BF)


def contract(order, ys, weights, groups, transposed):
    layout = tuple(len(w) for w in weights)
    nb = len(weights) // groups
    subs, _, sub_rows, ff = ys[0].shape
    rows = subs * sub_rows
    return local_call(
        functools.partial(contract_kernel, layout, groups, transposed),
        [order, *ys, *(v for w in weights for v in w)],
        [jax.ShapeDtypeStruct((rows, nb * BLOCK), BF)] * 4,
        [pltpu.VMEM((4 * rows, nb * BLOCK), F32)],
        8 * rows * nb * BLOCK * groups * ff,
        sum(layout),
    )


def factor_kernel(members, place_ref, near_ref, far_ref, *refs):
    rights, outs, (held,) = taken(refs, (len(members), 4, 1))
    first = place_ref[1] == 0
    for i, degree in enumerate(members):
        right = rights[i][...]
        for j in range(2):
            near = near_ref[degree + j * SECTIONS]
            far = far_ref[degree + j * SECTIONS]
            left = jnp.concatenate(
                [jnp.where(first, near, far), jnp.where(first, far, near)], axis=0
            )
            held[2 * i + j] = t_dot(left, right).astype(BF)
    part = BLOCK // 4
    for k in range(4):
        at = pl.multiple_of((place_ref[0] ^ k) * part, part)
        outs[k][...] = held[:, pl.ds(at, part), :]


def factor_parts(place, members, near, far, rights):
    count = 2 * len(members)
    return local_call(
        functools.partial(factor_kernel, members),
        [place, near, far, *rights],
        [jax.ShapeDtypeStruct((count, BLOCK // 4, BLOCK), BF)] * 4,
        [pltpu.VMEM((count, BLOCK, BLOCK), BF)],
        2 * count * rights[0].shape[0] * BLOCK * BLOCK,
    )


def stack_kernel(_, *refs):
    for i, ref in enumerate(refs[:-1]):
        refs[-1][i] = ref[...]


def place_kernel(place_ref, *refs):
    part = BLOCK // 4
    *pieces, self_ref, cross_ref = refs
    for b, members in enumerate(BATCHES):
        for k in range(4):
            at = pl.multiple_of((place_ref[0] ^ k) * part, part)
            for i, degree in enumerate(members):
                self_ref[degree, pl.ds(at, part), :] = f32(pieces[4 * b + k][2 * i])
                cross_ref[degree, pl.ds(at, part), :] = f32(pieces[4 * b + k][2 * i + 1])


def body(tokens, gate_weight, up_weight, down_weight, factor_self, factor_cross, cotangent):
    h, x, y, lh, ll, c = (lax.axis_index(a) for a in (*DP, *MP))
    order = (x ^ y).astype(jnp.int32).reshape(1)
    place = jnp.stack([x, h]).astype(jnp.int32)
    rows = tokens.shape[0]
    n = rows // 4
    ff = gate_weight.shape[1]

    half = BLOCK // 2
    gate_far = [swap(gate_weight[:half], "ll")]
    gate_near = swap(gate_weight, "c")
    up_near = swap(up_weight, "c")
    down_near = swap(down_weight, "c")
    gate_far.append(swap(gate_weight[half:], "ll"))
    up_far = [swap(up_weight[:half], "ll"), swap(up_weight[half:], "ll")]

    halved = cotangent.reshape(2, 2 * n, BLOCK)
    cot = jnp.concatenate([pick(halved, c), swap(pick(halved, 1 - c), "c")], axis=1)
    cot = by_pair(cot, swap(cot, "h"), h)
    cots = gather4(cot.reshape(4 * n, 2 * BLOCK), "x")
    terms = expand(order, cots, [[down_weight], [down_near]], 1, 1, True)

    current = tokens
    inputs = []
    partners = []
    for degree in range(SECTIONS):
        axis, bits = PARTNER[degree]
        partner = swap(current, axis, bits)
        inputs.append(current)
        partners.append(partner)
        result = dot(current, factor_self[degree]) + dot(partner, factor_cross[degree])
        current = result.astype(BF)

    count = 2 * SECTIONS
    shape = jax.ShapeDtypeStruct((count, rows, BLOCK), BF)
    (saved,) = local_call(stack_kernel, [place, *inputs, *partners], [shape], [], 0)
    saved_far = swap(saved, "h")

    quarters = current.reshape(2, 2, n, BLOCK)

    def quarter(dc, dl):
        return pick(pick(quarters, c ^ dc), ll ^ dl)

    mine = jnp.concatenate(
        [
            quarter(0, 0),
            swap(quarter(1, 0), "c"),
            swap(quarter(0, 1), "ll"),
            swap(quarter(1, 1), ("ll", "c"), 3),
        ],
        axis=1,
    )
    mine, *far = tie(mine, *gate_far, *up_far)
    gate_far, up_far = far[:2], far[2:]
    mine = by_pair(mine, swap(mine, "h"), h).reshape(2 * n, 4 * BLOCK)
    rotated = gather4(mine, "x")
    gate_cross = [swap(v, "c") for v in gate_far]
    up_cross = [swap(v, "c") for v in up_far]
    gates = [[gate_weight], [gate_near], gate_far, gate_cross]
    ups = [[up_weight], [up_near], up_far, up_cross]
    sums = expand(order, rotated, gates + ups, 2, 2, False)

    sums = sent4(sums, "y")
    sums[0], *terms = tie(sums[0], *sent4(terms, "y"))
    hid = summed(terms).reshape(2, 2, n, ff)
    hid = halves(hid, "lh", lh)
    hidden_grad = halves(hid, "ll", ll)
    sums = halves(summed(sums), "lh", lh)
    gate_sum = sums[0]
    up_sum = sums[1]

    logistic = jax.nn.sigmoid(gate_sum)
    hidden = (gate_sum * logistic * up_sum).astype(BF)
    gate_grad = hidden_grad * up_sum * logistic * (1.0 + gate_sum * (1.0 - logistic))
    up_grad = hidden_grad * gate_sum * logistic
    grads = jnp.stack([gate_grad.astype(BF), up_grad.astype(BF)])

    grads = by_pair(grads, swap(grads, "lh"), lh)
    grads = gather4(grads, "y")
    hidden_far, grads[1] = tie(swap(hidden, "lh"), grads[1])
    hidden = by_pair(hidden, hidden_far, lh)
    hidden = by_pair(hidden, swap(hidden, "ll"), ll).reshape(4, 1, n, ff)
    hiddens = gather4(hidden, "y")
    terms = contract(order, grads, gates + ups, 2, True)

    total = scatter4(terms, "x").astype(BF)
    total = (f32(total) + f32(swap(total, "h"))).astype(BF)
    blocks = [total[:, i * BLOCK : (i + 1) * BLOCK].reshape(2, n, BLOCK) for i in range(4)]
    near = by_pair(blocks[0], swap(blocks[2], "ll"), ll, 1)
    far = by_pair(swap(blocks[1], "c"), swap(blocks[3], ("ll", "c"), 3), ll, 1)
    gradient = by_pair(near, far, c, 1).reshape(2 * rows, BLOCK)

    mixed = contract(order, hiddens, [[down_weight], [down_near]], 1, False)
    mixed = sent4(mixed, "x")

    ws = [None] * SECTIONS
    for degree in reversed(range(SECTIONS)):
        axis, bits = PARTNER[degree]
        ws[degree] = gradient
        carried = dot_t(gradient, factor_cross[degree]).astype(BF)
        returned = swap(carried, axis, bits)
        if degree == 2:
            returned, *mixed = tie(returned, *mixed)
            mixed = summed(mixed).reshape(2, 2, n, 2 * BLOCK)
            mixed_far = swap(pick(mixed, 1 - h, 1).astype(BF), "h")
        direct = dot_t(gradient, factor_self[degree])
        gradient = (direct + f32(returned)).astype(BF)
    input_grad = pick(gradient.reshape(2, rows, BLOCK), h)

    early, late = [
        factor_parts(place, members, saved, saved_far, [ws[d] for d in members])
        for members in BATCHES
    ]
    early = sent4(early, "x")
    late[0], mixed_far, *early = tie(late[0], mixed_far, *early)
    late = summed(sent4(late, "x")).astype(BF)
    pieces = gather4(summed(early).astype(BF), "x") + gather4(late, "x")
    out = jax.ShapeDtypeStruct(factor_self.shape, F32)
    self_grad, cross_grad = local_call(place_kernel, [place, *pieces], [out, out], [], 0)

    mixed = (pick(mixed, h, 1) + f32(mixed_far)).astype(BF)
    other = swap(mixed[:, :, BLOCK:], "c")
    mixed_out = by_pair(mixed[:, :, :BLOCK], other, c).reshape(rows, BLOCK)

    return (mixed_out, input_grad, self_grad, cross_grad)


def solution(mesh):
    finer = Mesh(mesh.devices.reshape(2, 4, 4, 2, 2, 2), (*DP, *MP))
    in_specs = (
        P(DP, MP),
        P(MP, DP),
        P(MP, DP),
        P(DP, MP),
        P(None, MP, None),
        P(None, MP, None),
        P(DP, MP),
    )
    out_specs = (P(DP, MP), P(DP, MP), P(None, MP, None), P(None, MP, None))
    return jax.shard_map(body, mesh=finer, in_specs=in_specs, out_specs=out_specs, check_vma=False)
```

```python
import functools

import jax
import jax.numpy as jnp
from jax import lax
from jax.experimental import pallas as pl
from jax.experimental.pallas import tpu as pltpu
from jax.sharding import Mesh
from jax.sharding import PartitionSpec as P


BLOCK = 256
SECTIONS = 5
TILE = 256
GRANT = 60 * 1024 * 1024
PARTS = ((0, 3), (3, 7))
DP = ("h", "x")
MP = ("y", "lh", "ll", "c")
BF = jnp.bfloat16
F32 = jnp.float32
PARTNER = (("c", 1), ("ll", 1), ("lh", 1), ("y", 1), ("y", 2))
BATCHES = ((4, 3, 2), (1, 0))


def swap(value, axis, bits=1):
    count = lax.axis_size(axis)
    return lax.ppermute(value, axis, [(i, i ^ bits) for i in range(count)])


def pick(value, index, dim=0):
    return lax.dynamic_index_in_dim(value, index, dim, keepdims=False)


def dot(a, b):
    return jnp.dot(a, b, preferred_element_type=F32)


def dot_t(a, b):
    return lax.dot_general(a, b, (((1,), (1,)), ((), ())), preferred_element_type=F32)


def t_dot(a, b):
    return lax.dot_general(a, b, (((0,), (0,)), ((), ())), preferred_element_type=F32)


def f32(v):
    return v.astype(F32)


def tie(*values):
    return lax.optimization_barrier(values)


def gather4(value, axis):
    return [value] + [swap(value, axis, k) for k in (1, 2, 3)]


def sent4(parts, axis):
    return [parts[0]] + [swap(parts[k], axis, k) for k in (1, 2, 3)]


def summed(parts):
    total = f32(parts[0])
    for v in parts[1:]:
        total = total + f32(v)
    return total


def scatter4(parts, axis):
    return summed(sent4(parts, axis))


def halves(parts, axis, mine):
    other = swap(pick(parts, 1 - mine).astype(BF), axis)
    return pick(parts, mine) + f32(other)


def by_pair(own, other, index, dim=0):
    return jnp.stack(
        [jnp.where(index == 0, own, other), jnp.where(index == 0, other, own)], axis=dim
    )


VMEM = pl.BlockSpec(memory_space=pltpu.VMEM)
SMEM = pl.BlockSpec(memory_space=pltpu.SMEM)


def local_call(kernel, operands, out_shape, scratch, flops, fetched=0, placed=0):
    moving = fetched + placed
    if fetched:
        arrays = operands[1 : 1 + fetched]
        scratch = [
            *scratch,
            *(pltpu.VMEM(v.shape, v.dtype) for v in arrays),
            pltpu.SemaphoreType.DMA((len(PARTS), fetched)),
        ]
    moved = sum(v.size * v.dtype.itemsize for v in (*operands[1:], *out_shape))
    out = pl.pallas_call(
        kernel,
        in_specs=[SMEM]
        + [pl.BlockSpec(memory_space=pl.ANY)] * moving
        + [VMEM] * (len(operands) - 1 - moving),
        out_specs=[VMEM] * len(out_shape),
        out_shape=out_shape,
        scratch_shapes=scratch,
        cost_estimate=pl.CostEstimate(flops=flops, bytes_accessed=moved, transcendentals=0),
        compiler_params=pltpu.CompilerParams(vmem_limit_bytes=GRANT),
    )(*operands)
    return list(out)


def taken(refs, counts):
    out = []
    for count in counts:
        out.append(refs[:count])
        refs = refs[count:]
    return out


def block_of(refs, index):
    parts = [r[index] for r in refs]
    return parts[0] if len(parts) == 1 else jnp.concatenate(parts, axis=0)


def fetch(sources, targets, sems, across):
    copies = []
    for p, (low, high) in enumerate(PARTS):
        units = slice(low * TILE, high * TILE)
        copies.append([])
        for i, (v, to) in enumerate(zip(sources, targets)):
            index = (*[slice(None)] * (len(v.shape) - 1), units) if across[i] else (units,)
            copies[p].append(pltpu.make_async_copy(v.at[index], to.at[index], sems.at[p, i]))
    for part in copies:
        for copy in part:
            copy.start()

    def arrived(p):
        for copy in copies[p]:
            copy.wait()

    return arrived


def expand_kernel(layout, groups, transposed, order_ref, *refs):
    count = sum(layout)
    sources, xs, outs, (held, x_sems), flat, (sems,) = taken(refs, (count, 4, 4, 2, count, 1))
    rows = xs[0].shape[0]
    lefts = []
    for k in range(4):
        at = pl.multiple_of((order_ref[0] ^ k) * rows, rows)
        copy = pltpu.make_async_copy(xs[k], held.at[pl.ds(at, rows), :], x_sems.at[k])
        copy.start()
        lefts.append(copy)
    arrived = fetch(sources, flat, sems, [not transposed] * count)
    for copy in lefts:
        copy.wait()
    ws = taken(flat, layout)
    nb = len(ws) // groups
    subs, _, sub_rows, _ = outs[0].shape

    def step(t):
        tile = pl.ds(pl.multiple_of(t * TILE, TILE), TILE)
        index = (tile, slice(None)) if transposed else (slice(None), tile)
        for g in range(groups):
            total = None
            for i in range(nb):
                left = held[:, i * BLOCK : (i + 1) * BLOCK]
                right = block_of(ws[g * nb + i], index)
                part = dot_t(left, right) if transposed else dot(left, right)
                total = part if total is None else total + part
            total = total.astype(BF)
            for j in range(4):
                for s in range(subs):
                    at = j * rows + s * sub_rows
                    outs[j][s, g, :, tile] = total[at : at + sub_rows]

    for p, (low, high) in enumerate(PARTS):
        arrived(p)
        pl.loop(low, high)(step)


def expand(order, xs, weights, groups, subs, transposed):
    layout = tuple(len(w) for w in weights)
    nb = len(weights) // groups
    rows = xs[0].shape[0]
    ff = weights[0][0].shape[0 if transposed else 1]
    return local_call(
        functools.partial(expand_kernel, layout, groups, transposed),
        [order, *(v for w in weights for v in w), *xs],
        [jax.ShapeDtypeStruct((subs, groups, rows // subs, ff), BF)] * 4,
        [pltpu.VMEM((4 * rows, nb * BLOCK), BF), pltpu.SemaphoreType.DMA((4,))],
        8 * rows * nb * BLOCK * groups * ff,
        sum(layout),
        4,
    )


def contract_kernel(layout, groups, transposed, order_ref, *refs):
    count = sum(layout)
    far_ys, sources, outs, (total,), ys, flat, (sems,) = taken(
        refs, (4, count, 4, 1, 4, count, 1)
    )
    across = [True] * 4 + [transposed] * count
    arrived = fetch([*far_ys, *sources], [*ys, *flat], sems, across)
    ws = taken(flat, layout)
    nb = len(ws) // groups
    rows = outs[0].shape[0]
    subs, _, _, _ = ys[0].shape
    total[...] = jnp.zeros_like(total)

    def step(t):
        tile = pl.ds(pl.multiple_of(t * TILE, TILE), TILE)
        index = (slice(None), tile) if transposed else (tile, slice(None))
        lefts = [
            jnp.concatenate(
                [ys[j][s, g, :, tile] for j in range(4) for s in range(subs)], axis=0
            )
            for g in range(groups)
        ]
        for i in range(nb):
            out = None
            for g in range(groups):
                right = block_of(ws[g * nb + i], index)
                part = dot_t(lefts[g], right) if transposed else dot(lefts[g], right)
                out = part if out is None else out + part
            total[:, i * BLOCK : (i + 1) * BLOCK] += out

    for p, (low, high) in enumerate(PARTS):
        arrived(p)
        pl.loop(low, high)(step)

    for k in range(4):
        at = pl.multiple_of((order_ref[0] ^ k) * rows, rows)
        outs[k][...] = total[pl.ds(at, rows), :].astype(BF)


def contract(order, ys, weights, groups, transposed):
    layout = tuple(len(w) for w in weights)
    nb = len(weights) // groups
    subs, _, sub_rows, ff = ys[0].shape
    rows = subs * sub_rows
    return local_call(
        functools.partial(contract_kernel, layout, groups, transposed),
        [order, *ys, *(v for w in weights for v in w)],
        [jax.ShapeDtypeStruct((rows, nb * BLOCK), BF)] * 4,
        [pltpu.VMEM((4 * rows, nb * BLOCK), F32)],
        8 * rows * nb * BLOCK * groups * ff,
        4 + sum(layout),
    )


def factor_kernel(members, place_ref, near_ref, far_ref, *refs):
    rights, outs, (held,) = taken(refs, (len(members), 4, 1))
    first = place_ref[1] == 0
    for i, degree in enumerate(members):
        right = rights[i][...]
        for j in range(2):
            near = near_ref[degree + j * SECTIONS]
            far = far_ref[degree + j * SECTIONS]
            left = jnp.concatenate(
                [jnp.where(first, near, far), jnp.where(first, far, near)], axis=0
            )
            held[2 * i + j] = t_dot(left, right).astype(BF)
    part = BLOCK // 4
    for k in range(4):
        at = pl.multiple_of((place_ref[0] ^ k) * part, part)
        outs[k][...] = held[:, pl.ds(at, part), :]


def factor_parts(place, members, near, far, rights):
    count = 2 * len(members)
    return local_call(
        functools.partial(factor_kernel, members),
        [place, near, far, *rights],
        [jax.ShapeDtypeStruct((count, BLOCK // 4, BLOCK), BF)] * 4,
        [pltpu.VMEM((count, BLOCK, BLOCK), BF)],
        2 * count * rights[0].shape[0] * BLOCK * BLOCK,
    )


def stack_kernel(_, *refs):
    for i, ref in enumerate(refs[:-1]):
        refs[-1][i] = ref[...]


def place_kernel(place_ref, *refs):
    part = BLOCK // 4
    *pieces, self_ref, cross_ref = refs
    for b, members in enumerate(BATCHES):
        for k in range(4):
            at = pl.multiple_of((place_ref[0] ^ k) * part, part)
            for i, degree in enumerate(members):
                self_ref[degree, pl.ds(at, part), :] = f32(pieces[4 * b + k][2 * i])
                cross_ref[degree, pl.ds(at, part), :] = f32(pieces[4 * b + k][2 * i + 1])


def body(tokens, gate_weight, up_weight, down_weight, factor_self, factor_cross, cotangent):
    h, x, y, lh, ll, c = (lax.axis_index(a) for a in (*DP, *MP))
    order = (x ^ y).astype(jnp.int32).reshape(1)
    place = jnp.stack([x, h]).astype(jnp.int32)
    rows = tokens.shape[0]
    n = rows // 4
    ff = gate_weight.shape[1]

    half = BLOCK // 2
    gate_far = [swap(gate_weight[:half], "ll")]
    gate_near = swap(gate_weight, "c")
    up_near = swap(up_weight, "c")
    down_near = swap(down_weight, "c")
    gate_far.append(swap(gate_weight[half:], "ll"))
    up_far = [swap(up_weight, "ll")]

    halved = cotangent.reshape(2, 2 * n, BLOCK)
    cot = jnp.concatenate([pick(halved, c), swap(pick(halved, 1 - c), "c")], axis=1)
    cot = by_pair(cot, swap(cot, "h"), h)
    cots = gather4(cot.reshape(4 * n, 2 * BLOCK), "x")
    terms = expand(order, cots, [[down_weight], [down_near]], 1, 1, True)

    current = tokens
    inputs = []
    partners = []
    for degree in range(SECTIONS):
        axis, bits = PARTNER[degree]
        partner = swap(current, axis, bits)
        inputs.append(current)
        partners.append(partner)
        result = dot(current, factor_self[degree]) + dot(partner, factor_cross[degree])
        current = result.astype(BF)

    count = 2 * SECTIONS
    shape = jax.ShapeDtypeStruct((count, rows, BLOCK), BF)
    (saved,) = local_call(stack_kernel, [place, *inputs, *partners], [shape], [], 0)
    saved_far = swap(saved, "h")

    quarters = current.reshape(2, 2, n, BLOCK)

    def quarter(dc, dl):
        return pick(pick(quarters, c ^ dc), ll ^ dl)

    mine = jnp.concatenate(
        [
            quarter(0, 0),
            swap(quarter(1, 0), "c"),
            swap(quarter(0, 1), "ll"),
            swap(quarter(1, 1), ("ll", "c"), 3),
        ],
        axis=1,
    )
    mine, *gate_far = tie(mine, *gate_far)
    mine = by_pair(mine, swap(mine, "h"), h).reshape(2 * n, 4 * BLOCK)
    rotated = gather4(mine, "x")
    rotated[2], *up_far = tie(rotated[2], *up_far)
    gate_cross = [swap(v, "c") for v in gate_far]
    up_cross = [swap(v, "c") for v in up_far]
    gates = [[gate_weight], [gate_near], gate_far, gate_cross]
    ups = [[up_weight], [up_near], up_far, up_cross]
    sums = expand(order, rotated, gates + ups, 2, 2, False)

    sums = sent4(sums, "y")
    sums[0], *terms = tie(sums[0], *sent4(terms, "y"))
    hid = summed(terms).reshape(2, 2, n, ff)
    hid = halves(hid, "lh", lh)
    hidden_grad = halves(hid, "ll", ll)
    sums = halves(summed(sums), "lh", lh)
    gate_sum = sums[0]
    up_sum = sums[1]

    logistic = jax.nn.sigmoid(gate_sum)
    hidden = (gate_sum * logistic * up_sum).astype(BF)
    gate_grad = hidden_grad * up_sum * logistic * (1.0 + gate_sum * (1.0 - logistic))
    up_grad = hidden_grad * gate_sum * logistic
    grads = jnp.stack([gate_grad.astype(BF), up_grad.astype(BF)])

    grads = by_pair(grads, swap(grads, "lh"), lh)
    grads = gather4(grads, "y")
    hidden_far, grads[1] = tie(swap(hidden, "lh"), grads[1])
    hidden = by_pair(hidden, hidden_far, lh)
    hidden = by_pair(hidden, swap(hidden, "ll"), ll).reshape(4, 1, n, ff)
    hiddens = gather4(hidden, "y")
    terms = contract(order, grads, gates + ups, 2, True)

    total = scatter4(terms, "x").astype(BF)
    total = (f32(total) + f32(swap(total, "h"))).astype(BF)
    blocks = [total[:, i * BLOCK : (i + 1) * BLOCK].reshape(2, n, BLOCK) for i in range(4)]
    near = by_pair(blocks[0], swap(blocks[2], "ll"), ll, 1)
    far = by_pair(swap(blocks[1], "c"), swap(blocks[3], ("ll", "c"), 3), ll, 1)
    gradient = by_pair(near, far, c, 1).reshape(2 * rows, BLOCK)

    mixed = contract(order, hiddens, [[down_weight], [down_near]], 1, False)
    mixed = sent4(mixed, "x")

    ws = [None] * SECTIONS
    for degree in reversed(range(SECTIONS)):
        axis, bits = PARTNER[degree]
        ws[degree] = gradient
        carried = dot_t(gradient, factor_cross[degree]).astype(BF)
        returned = swap(carried, axis, bits)
        if degree == 2:
            returned, *mixed = tie(returned, *mixed)
            mixed = summed(mixed).reshape(2, 2, n, 2 * BLOCK)
            mixed_far = swap(pick(mixed, 1 - h, 1).astype(BF), "h")
        direct = dot_t(gradient, factor_self[degree])
        gradient = (direct + f32(returned)).astype(BF)
    input_grad = pick(gradient.reshape(2, rows, BLOCK), h)

    early, late = [
        factor_parts(place, members, saved, saved_far, [ws[d] for d in members])
        for members in BATCHES
    ]
    early = sent4(early, "x")
    late[0], mixed_far, *early = tie(late[0], mixed_far, *early)
    late = summed(sent4(late, "x")).astype(BF)
    pieces = gather4(summed(early).astype(BF), "x") + gather4(late, "x")
    out = jax.ShapeDtypeStruct(factor_self.shape, F32)
    self_grad, cross_grad = local_call(place_kernel, [place, *pieces], [out, out], [], 0)

    mixed = (pick(mixed, h, 1) + f32(mixed_far)).astype(BF)
    other = swap(mixed[:, :, BLOCK:], "c")
    mixed_out = by_pair(mixed[:, :, :BLOCK], other, c).reshape(rows, BLOCK)

    return (mixed_out, input_grad, self_grad, cross_grad)


def solution(mesh):
    finer = Mesh(mesh.devices.reshape(2, 4, 4, 2, 2, 2), (*DP, *MP))
    in_specs = (
        P(DP, MP),
        P(MP, DP),
        P(MP, DP),
        P(DP, MP),
        P(None, MP, None),
        P(None, MP, None),
        P(DP, MP),
    )
    out_specs = (P(DP, MP), P(DP, MP), P(None, MP, None), P(None, MP, None))
    return jax.shard_map(body, mesh=finer, in_specs=in_specs, out_specs=out_specs, check_vma=False)
```
